32 devices in a mesh: tile: 16 (over z, y, x), band: 2 (over core).
Axes of the slice: x: 2, y: 2, z: 4, core: 2. Of those that a mesh axis runs over, the one named last changes fastest.
Arguments:
- column_state: float32 [6, 8, 8, 4096], P(None, None, 'band', 'tile'), may hold values from -6 to 6
- conv_flags: int32 [8, 4096], P('band', 'tile'), may hold values 0 or 1
- block_counts: int32 [2, 16], P('band', 'tile'), may hold values from 0 to 4, as said below
- diffusion: float32 [6, 8], replicated, may hold values from 0.02 to 0.2
- w_embed: bfloat16 [6, 256], replicated, may hold values from -2.5 to 2.5
- level_embed: bfloat16 [8, 256], replicated, may hold values from -3 to 3
- norm_gains: float32 [3, 256], replicated, may hold values from 0.1 to 1.9
- w_qkv: bfloat16 [256, 768], replicated, may hold values from -0.375 to 0.375
- w_out: bfloat16 [256, 256], replicated, may hold values from -0.375 to 0.375
- w_up: bfloat16 [256, 1024], replicated, may hold values from -0.375 to 0.375
- w_down: bfloat16 [1024, 256], replicated, may hold values from -0.1875 to 0.1875
- w_head: bfloat16 [256, 6], replicated, may hold values from -0.375 to 0.375
Outputs:
- new_state: float32 [6, 8, 8, 4096], P(None, None, 'band', 'tile')
The draws below stay inside these ranges and needn't reach their ends.
Inputs may be any that keep to these rules, and one draw needn't show every extreme that they name: `block_counts`: every device has 0, 1 or 4 active blocks. In each band, no two devices with 4 active blocks lie 1, 2, or half the number of tiles plus or minus 1 tiles apart, counted round the tile axis.
All inputs are finite; a program needn't handle non-finite values. No bound on the sum of `conv_flags` on one device may be relied on, other than what follows from the above.
Results may differ from the reference program's by a relative error of at most 0.0031.
Values may be sent and summed in bfloat16 or wider, within the bound.
No kernel may reach another device: no remote copies, remote signals or barrier semaphores. Data moves between devices by JAX's collectives and lax.ppermute only.
A program may use at most 64 MiB of HBM per device.

```python
import math
import jax
import jax.numpy as jnp
from jax import lax

F = 6
L = 8
W = 256
FFH = 1024
HEADS = 4
CX = 256
CY = 4
NX = 4096
NY = 8
N_TILE = 16
N_BAND = 2


def draw_block_counts(key, part):
    key_base, key_heavy, key_light = jax.random.split(jax.random.fold_in(key, 11), 3)
    base = jax.random.randint(key_base, (N_BAND, 1), 0, N_TILE)
    tile_ids = jnp.arange(N_TILE, dtype=jnp.int32)[None, :]
    relative = (tile_ids - base) % N_TILE
    candidate = (relative % 3 == 0) & (relative <= N_TILE // 2 - 2)
    heavy = candidate & ((jax.random.randint(key_heavy, (N_BAND, N_TILE), 0, 4) > 0) | (relative == 0))
    light_count = jax.random.randint(key_light, (N_BAND, N_TILE), 0, 2)
    light_count = jnp.where(relative == 1, 1, light_count)
    light_count = jnp.where(relative == 2, 0, light_count)
    result = jnp.where(heavy, CY, light_count)
    return result.astype(jnp.int32)


def plant(array, rng, least, largest):
    spot = [jax.random.randint(jax.random.fold_in(rng, axis), (), 0, length) for axis, length in enumerate(array.shape)]
    longest = array.shape.index(max(array.shape))
    neighbour = spot[:longest] + [(spot[longest] + 1) % array.shape[longest]] + spot[longest + 1:]
    return array.at[tuple(spot)].set(least).at[tuple(neighbour)].set(largest)


def shard_levels(rng, shape, shards, smallest, high):
    factor_of = 1.0
    for dim, shards_of in shards:
        draws = jax.random.uniform(jax.random.fold_in(jax.random.fold_in(rng, 6), dim), (shards_of,), jnp.float32, smallest / len(shards), high / len(shards))
        factor_of = factor_of * jnp.repeat(jnp.exp(draws), shape[dim] // shards_of).reshape((-1,) + (1,) * (len(shape) - 1 - dim))
    return factor_of


def gaussian(stream_key, extent, spread, limit, cuts=(), held_as=jnp.bfloat16):
    values = jax.random.normal(stream_key, extent, jnp.float32) * spread
    if len(cuts) > 0:
        values = shard_levels(stream_key, extent, cuts, -0.22, 0.18) * values
    return jnp.clip(values, min=-limit, max=limit).astype(held_as)


def setup_inputs(seed: int = 0) -> dict:
    seeds = jax.random.split(jax.random.key(seed), 13)
    return {
        "column_state": gaussian(seeds[0], (F, L, NY, NX), 1.0, 6.0, ((2, 2), (3, 16)), jnp.float32),
        "conv_flags": plant((jax.random.randint(seeds[1], (NY, NX), 0, 2) < 1).astype(jnp.int32), jax.random.fold_in(seeds[1], 1), 0, 1),
        "block_counts": draw_block_counts(jax.random.fold_in(seeds[12], 71), 0),
        "diffusion": jnp.clip(jnp.exp(jax.random.uniform(seeds[3], (F, L), jnp.float32, math.log(0.02), math.log(0.2))), 0.02, 0.2),
        "w_embed": gaussian(seeds[4], (F, W), F ** -0.5, 2.5),
        "level_embed": gaussian(seeds[5], (L, W), 0.5, 3.0),
        "norm_gains": jnp.clip(1.0 + 0.18 * jax.random.normal(seeds[6], (3, W), jnp.float32), 0.1, 1.9),
        "w_qkv": gaussian(seeds[7], (W, 3 * W), W ** -0.5, 0.375),
        "w_out": gaussian(seeds[8], (W, W), W ** -0.5, 0.375),
        "w_up": gaussian(seeds[9], (W, FFH), W ** -0.5, 0.375),
        "w_down": gaussian(seeds[10], (FFH, W), FFH ** -0.5, 0.1875),
        "w_head": gaussian(seeds[11], (W, F), W ** -0.5, 0.375),
    }


def rms_scale(values, gain):
    return values * lax.rsqrt(lax.optimization_barrier(jnp.mean(values * values, axis=-1, keepdims=True)) + 1e-05) * gain

def column_net(columns, w_embed, level_embed, norm_gains, w_qkv, w_out, w_up, w_down, w_head):
    highest = lax.Precision.HIGHEST
    levels = columns.shape[1]
    count_cols = columns.shape[2]
    model_width = w_out.shape[0]
    head_size = model_width // HEADS
    hidden_in = jnp.einsum('fln,fw->nlw', columns.astype(jnp.float32), w_embed.astype(jnp.float32), precision=highest)
    hidden_in = hidden_in + level_embed.astype(jnp.float32)[None]
    normed = rms_scale(hidden_in, norm_gains[0]).astype(jnp.bfloat16)
    projected = jnp.einsum('nlw,wk->nlk', normed.astype(jnp.float32), w_qkv.astype(jnp.float32), precision=highest).astype(jnp.bfloat16)
    queries = projected[:, :, :model_width].reshape(count_cols, levels, HEADS, head_size).astype(jnp.float32)
    keys_part = projected[:, :, model_width:2 * model_width].reshape(count_cols, levels, HEADS, head_size).astype(jnp.float32)
    values_part = projected[:, :, 2 * model_width:].reshape(count_cols, levels, HEADS, head_size).astype(jnp.float32)
    queries = queries * lax.rsqrt(lax.optimization_barrier(jnp.mean(queries * queries, axis=-1, keepdims=True)) + 1e-05)
    keys_part = keys_part * lax.rsqrt(lax.optimization_barrier(jnp.mean(keys_part * keys_part, axis=-1, keepdims=True)) + 1e-05)
    scores = jnp.einsum('nqhd,nkhd->nhqk', queries, keys_part, precision=highest) / math.sqrt(head_size)
    attention = jnp.exp(scores)
    attention = (attention / lax.optimization_barrier(jnp.sum(attention, axis=-1, keepdims=True))).astype(jnp.bfloat16)
    mixed_heads = jnp.einsum('nhqk,nkhd->nqhd', attention.astype(jnp.float32), values_part, precision=highest)
    mixed_heads = mixed_heads.astype(jnp.bfloat16).reshape(count_cols, levels, model_width)
    after_attn = hidden_in + jnp.einsum('nlw,wv->nlv', mixed_heads.astype(jnp.float32), w_out.astype(jnp.float32), precision=highest)
    normed_mlp = rms_scale(after_attn, norm_gains[1]).astype(jnp.bfloat16)
    inner_act = jax.nn.silu(jnp.einsum('nlw,wh->nlh', normed_mlp.astype(jnp.float32), w_up.astype(jnp.float32), precision=highest)).astype(jnp.bfloat16)
    after_mlp = after_attn + jnp.einsum('nlh,hw->nlw', inner_act.astype(jnp.float32), w_down.astype(jnp.float32), precision=highest)
    normed_out = rms_scale(after_mlp, norm_gains[2]).astype(jnp.bfloat16)
    return jnp.einsum('nlw,wf->fln', normed_out.astype(jnp.float32), w_head.astype(jnp.float32), precision=highest).astype(jnp.bfloat16)

def reference(column_state, conv_flags, block_counts, diffusion, w_embed, level_embed, norm_gains, w_qkv, w_out, w_up, w_down, w_head):
    padded_y = jnp.pad(column_state, ((0, 0), (0, 0), (1, 1), (0, 0)))
    laplace = jnp.roll(column_state, 1, axis=3) + jnp.roll(column_state, -1, axis=3)
    laplace = laplace + padded_y[:, :, 2:, :] + padded_y[:, :, :-2, :] - 4.0 * column_state
    dynamics_tend = diffusion[:, :, None, None] * laplace
    inputs = column_state.astype(jnp.bfloat16)
    blocked = inputs.reshape(F, L, NY, N_TILE, CX).transpose(2, 3, 0, 1, 4).reshape(NY * N_TILE, F, L, CX)
    row_ids = jnp.arange(NY, dtype=jnp.int32)
    active = (row_ids % CY)[:, None] < jnp.repeat(block_counts, CY, axis=0)

    def one_block(block_item):
        block_in, live_block = block_item
        return lax.cond(live_block, lambda block_arg: column_net(block_arg, w_embed, level_embed, norm_gains, w_qkv, w_out, w_up, w_down, w_head), lambda block_arg: jnp.zeros_like(block_arg), block_in)
    physics_blocks = lax.map(one_block, (blocked, active.reshape(-1)))
    physics_tend = physics_blocks.reshape(NY, N_TILE, F, L, CX).transpose(2, 3, 0, 1, 4).reshape(F, L, NY, NX).astype(jnp.float32)
    physics_mask = ((conv_flags == 1) & jnp.repeat(active, CX, axis=1)).astype(jnp.float32)
    return column_state + dynamics_tend + physics_mask * physics_tend
```

```python
import functools

import jax
import jax.numpy as jnp
from jax import lax
from jax.experimental import pallas as pl
from jax.experimental.pallas import tpu as pltpu
from jax.sharding import PartitionSpec as P

HEADS = 4
TILE = 32


def dot(a, b):
    return jnp.dot(a, b, preferred_element_type=jnp.float32)


def dot_nt(a, b):
    return lax.dot_general(a, b, (((1,), (1,)), ((), ())), preferred_element_type=jnp.float32)


def iota(shape, dim):
    return lax.broadcasted_iota(jnp.int32, shape, dim)


def rms(values, gain):
    mean = jnp.mean(values * values, axis=-1, keepdims=True)
    return values * lax.rsqrt(mean + 1e-05) * gain


def physics_kernel(
    count_ref,
    flags_ref,
    x_ref,
    embed_ref,
    level_ref,
    gains_ref,
    qkv_ref,
    out_w_ref,
    up_ref,
    down_ref,
    head_ref,
    phys_ref,
    inputs_sc,
    table_sc,
    pos_sc,
    heads_sc,
    tiles_sc,
):
    variables, levels, rows, cols = x_ref.shape
    width = out_w_ref.shape[0]
    head_size = width // HEADS
    pairs = variables * levels
    depth = inputs_sc.shape[1]
    tokens = levels * TILE
    half = width // 2
    bf16 = jnp.bfloat16

    count = count_ref[0, 0]
    live = (flags_ref[...] == 1) & (iota((rows, cols), 0) < count)
    live_f = jnp.where(live, 1.0, 0.0)
    before = jnp.where(iota((cols, cols), 0) < iota((cols, cols), 1), 1.0, 0.0).astype(bf16)
    pad = jnp.zeros((8 - rows, cols), jnp.float32)
    place = dot(jnp.concatenate([live_f, pad], axis=0).astype(bf16), before)
    pos_sc[...] = jnp.where(
        jnp.concatenate([live_f, pad], axis=0) > 0.5, place, -1.0
    ).astype(jnp.int32)
    for y in range(rows):
        tiles_sc[y] = (jnp.sum(live_f[y : y + 1, :]).astype(jnp.int32) + (TILE - 1)) // TILE

    tail_rows = iota((depth - pairs, cols), 0)
    tail = jnp.where(tail_rows < levels, 1.0, 0.0).astype(bf16)
    for y in range(rows):
        inputs_sc[y, :pairs, :] = x_ref[:, :, y, :].reshape(pairs, cols).astype(bf16)
        inputs_sc[y, pairs:, :] = tail
    phys_ref[...] = jnp.zeros(phys_ref.shape, phys_ref.dtype)
    for f in range(variables):
        table_sc[f * levels : (f + 1) * levels, :] = jnp.broadcast_to(
            embed_ref[f : f + 1, :].astype(jnp.float32), (levels, width)
        ).astype(bf16)
    table_sc[pairs : pairs + levels, :] = level_ref[...]
    table_sc[pairs + levels :, :] = jnp.zeros((depth - pairs - levels, width), bf16)
    heads_sc[...] = jnp.where(
        iota((width, width), 0) // head_size == iota((width, width), 1) // head_size,
        1.0 / head_size,
        0.0,
    ).astype(bf16)

    def one_tile(y, t):
        slots = iota((TILE, cols), 0) + t * TILE
        pick = jnp.where(pos_sc[pl.ds(y, 1), :] == slots, 1.0, 0.0).astype(bf16)
        packed = dot_nt(pick, inputs_sc[y]).astype(bf16)
        own_level = (iota((tokens, depth), 1) % levels) == (iota((tokens, depth), 0) // TILE)
        spread = jnp.where(own_level, jnp.concatenate([packed] * levels, axis=0), 0)
        hidden = dot(spread.astype(bf16), table_sc[...])

        normed = rms(hidden, gains_ref[0:1, :]).astype(bf16)
        queries = dot(normed, qkv_ref[:, :width])
        keys = dot(normed, qkv_ref[:, width : 2 * width])
        values = dot(normed, qkv_ref[:, 2 * width :]).astype(bf16)
        q_mean = dot((queries * queries).astype(bf16), heads_sc[...])
        k_mean = dot((keys * keys).astype(bf16), heads_sc[...])
        queries = (queries * (lax.rsqrt(q_mean + 1e-05) * head_size**-0.5)).astype(bf16)
        keys = (keys * lax.rsqrt(k_mean + 1e-05)).astype(bf16)
        head_of = iota((tokens, width), 1) // head_size
        same = (iota((tokens, tokens), 0) % TILE) == (iota((tokens, tokens), 1) % TILE)
        zero = jnp.zeros((), bf16)
        probs = []
        for h in range(HEADS):
            scores = dot_nt(jnp.where(head_of == h, queries, zero), keys)
            probs.append(jnp.where(same, jnp.exp(scores), 0.0).astype(bf16))
        mixed = []
        low = iota((tokens, half), 1) < head_size
        ones = jnp.ones((tokens, half), bf16)
        for side in range(2):
            part = values[:, side * half : (side + 1) * half]
            first = jnp.concatenate(
                [jnp.where(low, part, zero), jnp.where(low, ones, zero)], axis=1
            )
            second = jnp.concatenate(
                [jnp.where(low, zero, part), jnp.where(low, zero, ones)], axis=1
            )
            both = dot(probs[2 * side], first) + dot(probs[2 * side + 1], second)
            mixed.append(both[:, :half] / both[:, half:])
        mixed = jnp.concatenate(mixed, axis=1).astype(bf16)
        after_attn = hidden + dot(mixed, out_w_ref[...])

        normed = (rms(after_attn, gains_ref[1:2, :]) * 0.5).astype(bf16)
        inner = dot(normed, up_ref[...])
        inner = (inner + inner * jnp.tanh(inner)).astype(bf16)
        after_mlp = after_attn + dot(inner, down_ref[...])
        normed = rms(after_mlp, gains_ref[2:3, :]).astype(bf16)
        tend = dot_nt(head_ref[...], normed)
        level_of = (iota((levels, tokens), 1) // TILE) == iota((levels, tokens), 0)
        placed = jnp.concatenate(
            [
                jnp.where(level_of, jnp.broadcast_to(tend[f : f + 1, :], (levels, tokens)), 0.0)
                for f in range(variables)
            ],
            axis=0,
        ).astype(bf16)
        phys_ref[y] += dot(placed, jnp.concatenate([pick] * levels, axis=0))

    def one_row(y, carry):
        return lax.fori_loop(0, tiles_sc[y], lambda t, c: (one_tile(y, t), c)[1], carry)

    lax.fori_loop(0, rows, one_row, 0)


def physics(block_counts, conv_flags, column_state, weights):
    variables, levels, rows, cols = column_state.shape
    w_embed, level_embed, norm_gains, w_qkv, w_out, w_up, w_down, w_head = weights
    width = w_out.shape[0]
    depth = -(-(variables + 1) * levels // 64) * 64
    vmem = pl.BlockSpec(memory_space=pltpu.VMEM)
    return pl.pallas_call(
        physics_kernel,
        out_shape=jax.ShapeDtypeStruct((rows, variables * levels, cols), jnp.float32),
        in_specs=[pl.BlockSpec(memory_space=pltpu.SMEM)] + [vmem] * 10,
        out_specs=vmem,
        scratch_shapes=[
            pltpu.VMEM((rows, depth, cols), jnp.bfloat16),
            pltpu.VMEM((depth, width), jnp.bfloat16),
            pltpu.VMEM((8, cols), jnp.int32),
            pltpu.VMEM((width, width), jnp.bfloat16),
            pltpu.SMEM((rows,), jnp.int32),
        ],
        compiler_params=pltpu.CompilerParams(vmem_limit_bytes=24 << 20),
        cost_estimate=pl.CostEstimate(
            flops=6_000_000_000, bytes_accessed=2_000_000, transcendentals=4_000_000
        ),
        name="column_physics",
    )(
        block_counts,
        conv_flags,
        column_state,
        w_embed,
        level_embed,
        norm_gains,
        w_qkv,
        w_out,
        w_up,
        w_down,
        w_head.T,
    )


def padded(block, sides, width, periodic):
    for axis, dim in sides:
        count = lax.axis_size(axis)
        forward = [(i, i + 1) for i in range(count - 1)]
        if periodic:
            forward.append((count - 1, 0))
        backward = [(target, source) for source, target in forward]
        low = lax.ppermute(
            lax.slice_in_dim(block, block.shape[dim] - width, None, axis=dim), axis, forward
        )
        high = lax.ppermute(lax.slice_in_dim(block, 0, width, axis=dim), axis, backward)
        block = jnp.concatenate([low, block, high], axis=dim)
    return block


def shards(
    column_state,
    conv_flags,
    block_counts,
    diffusion,
    *weights,
):
    variables, levels, rows, cols = column_state.shape
    wide_x = padded(column_state.astype(jnp.bfloat16), (("tile", 3),), 1, True).astype(
        column_state.dtype
    )
    wide_y = padded(column_state.astype(jnp.bfloat16), (("band", 2),), 1, False).astype(
        column_state.dtype
    )
    laplace = wide_x[:, :, :, 2:] + wide_x[:, :, :, :-2]
    laplace = laplace + wide_y[:, :, 2:, :] + wide_y[:, :, :-2, :] - 4.0 * column_state
    dynamics_tend = diffusion[:, :, None, None] * laplace
    tend = physics(block_counts, conv_flags, column_state, weights)
    tend = tend.reshape(rows, variables, levels, cols).transpose(1, 2, 0, 3)
    return column_state + dynamics_tend + tend


def solution(mesh):
    placed = (
        P(None, None, "band", "tile"),
        P("band", "tile"),
        P("band", "tile"),
        P(),
        P(),
        P(),
        P(),
        P(),
        P(),
        P(),
        P(),
        P(),
    )
    return jax.shard_map(
        shards, mesh=mesh, in_specs=placed, out_specs=P(None, None, "band", "tile"), check_vma=False
    )
```

```python
import functools

import jax
import jax.numpy as jnp
from jax import lax
from jax.experimental import pallas as pl
from jax.experimental.pallas import tpu as pltpu
from jax.sharding import PartitionSpec as P

HEADS = 4
CHAIN = 32
CHAINS = 2
GROUP = 8
LANES = 128
bf16 = jnp.bfloat16
f32 = jnp.float32


def dot(a, b):
    return jnp.dot(a, b, preferred_element_type=f32)


def dot_nt(a, b):
    return lax.dot_general(a, b, (((1,), (1,)), ((), ())), preferred_element_type=f32)


def iota(shape, dim):
    return lax.broadcasted_iota(jnp.int32, shape, dim)


def rms(values, gain):
    mean = jnp.mean(values * values, axis=-1, keepdims=True)
    return values * lax.rsqrt(mean + 1e-05) * gain


def pack_kernel(band_ref, count_ref, flags_ref, x_ref, work_ref, give_ref, south_ref, north_ref, west_ref, east_ref):
    variables, levels, rows, cols = x_ref.shape
    pairs = variables * levels
    live = (flags_ref[...] == 1) & (iota((rows, cols), 0) < count_ref[0, 0])
    live = jnp.where(live, 1.0, 0.0)
    extra = work_ref.shape[0] - pairs
    west, east = [], []
    for y in range(rows):
        here = slice(y * cols, (y + 1) * cols)
        state = x_ref[:, :, y, :].reshape(pairs, cols)
        work_ref[:pairs, here] = state.astype(bf16)
        work_ref[pairs:, here] = jnp.where(
            iota((extra, cols), 0) == 0, live[y : y + 1, :], 0.0
        ).astype(bf16)
        west.append(state[:, :1])
        east.append(state[:, cols - 1 :])
    give_ref[...] = work_ref[:, rows * cols - give_ref.shape[1] :]
    first, last = work_ref[:pairs, :cols], work_ref[:pairs, (rows - 1) * cols :]
    if south_ref is None:
        north_ref[...] = jnp.where(band_ref[0, 0] == 0, last, first)
    else:
        north_ref[...] = last
        south_ref[...] = first
    lane = iota((pairs, LANES), 1)
    for ref, edges in ((west_ref, west), (east_ref, east)):
        total = jnp.zeros((pairs, LANES), f32)
        for y in range(rows):
            total = jnp.where(lane == y, edges[y], total)
        ref[...] = total.astype(bf16)


def network_kernel(
    phase,
    work_ref,
    got_ref,
    embed_ref,
    level_ref,
    gains_ref,
    qkv_ref,
    out_w_ref,
    up_ref,
    down_ref,
    head_ref,
    phys_ref,
    inputs_sc,
    table_sc,
    pos_sc,
    heads_sc,
):
    variables = embed_ref.shape[0]
    levels = level_ref.shape[0]
    width = out_w_ref.shape[0]
    cols = phys_ref.shape[1]
    given = got_ref.shape[1]
    head_size = width // HEADS
    pairs = variables * levels
    depth = inputs_sc.shape[0]
    tokens = levels * CHAIN
    group_tokens = levels * GROUP
    zero = jnp.zeros((), bf16)

    mask_rows = work_ref.shape[0] - pairs
    helping = jnp.max(got_ref[pairs:, :].astype(f32)) > 0.5

    def take(source, start):
        inputs_sc[:pairs, :] = source[:pairs, start : start + cols]
        pos_sc[...] = source[pairs : pairs + mask_rows, start : start + cols].astype(f32)

    if phase == 0:
        pl.when(helping)(lambda: take(got_ref, 0))
        pl.when(jnp.logical_not(helping))(lambda: take(work_ref, 0))
    else:
        pl.when(helping)(lambda: take(work_ref, 0))
        pl.when(jnp.logical_not(helping))(lambda: take(work_ref, given))
    inputs_sc[pairs:, :] = jnp.where(
        iota((depth - pairs, cols), 0) < levels, 1.0, 0.0
    ).astype(bf16)

    live = pos_sc[...]
    before = jnp.where(iota((cols, cols), 0) < iota((cols, cols), 1), 1.0, 0.0).astype(bf16)
    place = dot(live.astype(bf16), before)
    pos_sc[...] = jnp.where(live > 0.5, place, -1.0)
    total_live = jnp.sum(live).astype(jnp.int32)
    phys_ref[...] = jnp.zeros(phys_ref.shape, phys_ref.dtype)
    for f in range(variables):
        table_sc[f * levels : (f + 1) * levels, :] = jnp.broadcast_to(
            embed_ref[f : f + 1, :].astype(f32), (levels, width)
        ).astype(bf16)
    table_sc[pairs : pairs + levels, :] = level_ref[...]
    table_sc[pairs + levels :, :] = jnp.zeros((depth - pairs - levels, width), bf16)
    block_diag = iota((width, width), 0) // head_size == iota((width, width), 1) // head_size
    heads_sc[...] = jnp.where(block_diag, 1.0 / head_size, 0.0).astype(bf16)

    def embed(packed):
        lane_level = iota((levels, depth), 1) % levels
        parts = []
        for g in range(CHAIN // GROUP):
            rows_g = packed[g * GROUP : (g + 1) * GROUP, :]
            for l in range(levels):
                parts.append(jnp.where(lane_level == l, rows_g, 0.0))
        return dot(jnp.concatenate(parts, axis=0).astype(bf16), table_sc[...])

    def project(hidden):
        normed = rms(hidden, gains_ref[0:1, :]).astype(bf16)
        queries = dot(normed, qkv_ref[:, :width])
        keys = dot(normed, qkv_ref[:, width : 2 * width])
        values = dot(normed, qkv_ref[:, 2 * width :]).astype(bf16)
        return queries, keys, values

    def normalize(queries, keys):
        q_mean = dot((queries * queries).astype(bf16), heads_sc[...])
        k_mean = dot((keys * keys).astype(bf16), heads_sc[...])
        queries = (queries * (lax.rsqrt(q_mean + 1e-05) * head_size**-0.5)).astype(bf16)
        keys = (keys * lax.rsqrt(k_mean + 1e-05)).astype(bf16)
        return queries, keys

    def split(part):
        head_of = iota((group_tokens, width), 1) // head_size
        return jnp.concatenate(
            [jnp.where(head_of == h, part, zero) for h in range(HEADS)], axis=0
        )

    def attend(queries, keys, values):
        same = (iota((group_tokens, width), 0) % GROUP) == (iota((group_tokens, width), 1) % GROUP)
        probs, mixed = [], []
        for g in range(CHAIN // GROUP):
            here = slice(g * group_tokens, (g + 1) * group_tokens)
            scores = dot_nt(queries[here], split(keys[here]))
            prob = jnp.where(same, jnp.exp(scores), 0.0).astype(bf16)
            probs.append(prob)
            mixed.append(dot(prob, split(values[here])))
        total = dot(jnp.concatenate(probs, axis=0), heads_sc[...]) * head_size
        return (jnp.concatenate(mixed, axis=0) / total).astype(bf16)

    def feed(after_attn):
        normed = (rms(after_attn, gains_ref[1:2, :]) * 0.5).astype(bf16)
        inner = dot(normed, up_ref[...])
        inner = (inner + inner * jnp.tanh(inner)).astype(bf16)
        return after_attn + dot(inner, down_ref[...])

    def finish(after_mlp):
        normed = rms(after_mlp, gains_ref[2:3, :]).astype(bf16)
        tend = dot_nt(head_ref[...], normed)
        level_of = (iota((levels, tokens), 1) // GROUP) % levels == iota((levels, tokens), 0)
        return jnp.concatenate(
            [
                jnp.where(level_of, jnp.broadcast_to(tend[f : f + 1, :], (levels, tokens)), 0.0)
                for f in range(variables)
            ],
            axis=0,
        ).astype(bf16)

    def evaluate(start, chains):
        slots = (iota((chains * CHAIN, cols), 0) + start).astype(f32)
        pick = jnp.where(pos_sc[0:1, :] == slots, 1.0, 0.0)
        packed = dot_nt(pick.astype(bf16), inputs_sc[...])
        span = range(chains)
        hidden = [embed(packed[i * CHAIN : (i + 1) * CHAIN, :]) for i in span]
        qkv = [project(h) for h in hidden]
        qk = [normalize(q, k) for q, k, _ in qkv]
        mixed = [attend(qk[i][0], qk[i][1], qkv[i][2]) for i in span]
        after = [hidden[i] + dot(mixed[i], out_w_ref[...]) for i in span]
        after = [feed(a) for a in after]
        placed = jnp.concatenate([finish(a) for a in after], axis=1)
        parts = []
        for g in range(chains * CHAIN // GROUP):
            part = pick[g * GROUP : (g + 1) * GROUP, :]
            part = jnp.concatenate([part, part], axis=0).astype(bf16)
            parts.extend([part] * (levels // 2))
        phys_ref[...] += dot(placed, jnp.concatenate(parts, axis=0)).astype(phys_ref.dtype)

    units = (total_live + (CHAIN - 1)) // CHAIN
    rounds = units // CHAINS

    def body(t, carry):
        evaluate(t * (CHAIN * CHAINS), CHAINS)
        return carry

    lax.fori_loop(0, rounds, body, 0)
    lax.fori_loop(rounds * CHAINS, units, lambda t, c: (evaluate(t * CHAIN, 1), c)[1], 0)


def final_kernel(
    band_ref, bands, x_ref, diffusion_ref, work_ref, got_ref, a_ref, b_ref, back_ref,
    south_ref, north_ref, west_ref, east_ref, out_ref, phys_sc,
):
    variables, levels, rows, cols = x_ref.shape
    pairs = variables * levels
    whole = rows * cols
    na, nb = a_ref.shape[1], b_ref.shape[1]
    helping = jnp.max(got_ref[pairs:, :].astype(f32)) > 0.5

    @pl.when(helping)
    def _():
        phys_sc[:, :nb] = b_ref[...]
        phys_sc[:, nb:] = jnp.zeros((pairs, whole - nb), phys_sc.dtype)

    @pl.when(jnp.logical_not(helping))
    def _():
        phys_sc[:, :na] = a_ref[...]
        phys_sc[:, na : na + nb] = b_ref[...]
        phys_sc[:, na + nb :] = back_ref[...]

    level = iota((levels, levels), 0) == iota((levels, levels), 1)
    rate = jnp.concatenate(
        [
            jnp.sum(
                jnp.where(level, jnp.broadcast_to(diffusion_ref[f : f + 1, :], (levels, levels)), 0.0),
                axis=1,
                keepdims=True,
            )
            for f in range(variables)
        ],
        axis=0,
    )
    state = [x_ref[:, :, y, :].reshape(pairs, cols) for y in range(rows)]
    band = band_ref[0, 0]
    above = jnp.where(band > 0, north_ref[...].astype(f32), 0.0)
    below = jnp.where(band < bands - 1, south_ref[...].astype(f32), 0.0)
    lane = iota((pairs, cols), 1)
    for y in range(rows):
        here = state[y]
        left = jnp.where(lane == 0, west_ref[:, y : y + 1].astype(f32), pltpu.roll(here, 1, 1))
        right = jnp.where(
            lane == cols - 1, east_ref[:, y : y + 1].astype(f32), pltpu.roll(here, cols - 1, 1)
        )
        up = state[y - 1] if y > 0 else above
        down = state[y + 1] if y < rows - 1 else below
        laplace = left + right + up + down - 4.0 * here
        span = slice(y * cols, (y + 1) * cols)
        live = work_ref[pairs : pairs + 1, span].astype(f32) > 0.5
        tend = jnp.where(live, phys_sc[:, span].astype(f32), 0.0)
        out_ref[:, :, y, :] = (here + rate * laplace + tend).reshape(variables, levels, cols)


VMEM = pl.BlockSpec(memory_space=pltpu.VMEM)
SMEM = pl.BlockSpec(memory_space=pltpu.SMEM)


def shape(dims, dtype=bf16):
    return jax.ShapeDtypeStruct(dims, dtype)


def network(phase, cols, work, got, weights, dims):
    variables, levels = dims
    w_embed, level_embed, norm_gains, w_qkv, w_out, w_up, w_down, head_t = weights
    width = w_out.shape[0]
    pairs = variables * levels
    depth = -(-(pairs + levels) // 64) * 64
    return pl.pallas_call(
        functools.partial(network_kernel, phase),
        out_shape=shape((pairs, cols)),
        in_specs=[VMEM] * 10,
        out_specs=VMEM,
        scratch_shapes=[
            pltpu.VMEM((depth, cols), bf16),
            pltpu.VMEM((depth, width), bf16),
            pltpu.VMEM((work.shape[0] - pairs, cols), f32),
            pltpu.VMEM((width, width), bf16),
        ],
        compiler_params=pltpu.CompilerParams(vmem_limit_bytes=16 << 20),
        cost_estimate=pl.CostEstimate(
            flops=3_000_000_000, bytes_accessed=2_000_000, transcendentals=4_000_000
        ),
        name="column_physics",
    )(work, got, w_embed, level_embed, norm_gains, w_qkv, w_out, w_up, w_down, head_t)


def pack(band, block_counts, conv_flags, column_state, given, two_bands):
    variables, levels, rows, cols = column_state.shape
    pairs = variables * levels
    tall = pairs + 8
    row = shape((pairs, cols))
    edge = shape((pairs, LANES))
    outs = [shape((tall, rows * cols)), shape((tall, given))]
    outs += [row] if two_bands else [row, row]
    outs += [edge, edge]

    def kernel(*refs):
        if two_bands:
            refs = refs[:6] + (None,) + refs[6:]
        pack_kernel(*refs)

    return pl.pallas_call(
        kernel,
        out_shape=outs,
        in_specs=[SMEM, SMEM, VMEM, VMEM],
        out_specs=[VMEM] * len(outs),
        compiler_params=pltpu.CompilerParams(vmem_limit_bytes=8 << 20),
        name="pack",
    )(band, block_counts, conv_flags, column_state)


def physics(block_counts, conv_flags, column_state, weights):
    weights = weights[:-1] + (weights[-1].T,)
    band = jnp.zeros((1, 1), jnp.int32)
    work, give, *_ = pack(band, block_counts, conv_flags, column_state, 384, True)
    got = jnp.zeros_like(give)
    a = network(0, 384, work, got, weights, (6, 8))
    return a


def shards(column_state, conv_flags, block_counts, diffusion, *weights):
    variables, levels, rows, cols = column_state.shape
    pairs = variables * levels
    weights = weights[:-1] + (weights[-1].T,)
    tiles, bands = lax.axis_size("tile"), lax.axis_size("band")
    given = cols + cols // 2
    kept = rows * cols - 2 * given
    band = lax.axis_index("band").reshape(1, 1).astype(jnp.int32)
    packed = pack(band, block_counts, conv_flags, column_state, given, bands == 2)
    work, give = packed[:2]
    pairing = [(i, i ^ 1) for i in range(tiles)]
    got = lax.ppermute(give, "tile", pairing)
    if bands == 2:
        north = south = lax.ppermute(packed[2], "band", [(0, 1), (1, 0)])
    else:
        south = lax.ppermute(packed[2], "band", [(i + 1, i) for i in range(bands - 1)])
        north = lax.ppermute(packed[3], "band", [(i, i + 1) for i in range(bands - 1)])
    forward = [(i, (i + 1) % tiles) for i in range(tiles)]
    backward = [((i + 1) % tiles, i) for i in range(tiles)]
    east = lax.ppermute(packed[-2], "tile", backward)
    west = lax.ppermute(packed[-1], "tile", forward)
    a = network(0, given, work, got, weights, (variables, levels))
    back = lax.ppermute(a, "tile", pairing)
    b = network(1, kept, work, got, weights, (variables, levels))

    def kernel(band_ref, *refs):
        final_kernel(band_ref, bands, *refs)

    return pl.pallas_call(
        kernel,
        out_shape=shape(column_state.shape, f32),
        in_specs=[SMEM] + [VMEM] * 11,
        out_specs=VMEM,
        scratch_shapes=[pltpu.VMEM((pairs, rows * cols), bf16)],
        compiler_params=pltpu.CompilerParams(vmem_limit_bytes=8 << 20),
        name="combine",
    )(band, column_state, diffusion, work, got, a, b, back, south, north, west, east)


def solution(mesh):
    placed = (
        P(None, None, "band", "tile"),
        P("band", "tile"),
        P("band", "tile"),
        P(),
        P(),
        P(),
        P(),
        P(),
        P(),
        P(),
        P(),
        P(),
    )
    return jax.shard_map(
        shards, mesh=mesh, in_specs=placed, out_specs=P(None, None, "band", "tile"), check_vma=False
    )
```

```python
import functools

import jax
import jax.numpy as jnp
from jax import lax
from jax.experimental import pallas as pl
from jax.experimental.pallas import tpu as pltpu
from jax.sharding import PartitionSpec as P

HEADS = 4
CHAIN = 32
CHAINS = 4
GROUP = 8
LANES = 128
bf16 = jnp.bfloat16
f32 = jnp.float32


def dot(a, b):
    return jnp.dot(a, b, preferred_element_type=f32)


def dot_nt(a, b):
    return lax.dot_general(a, b, (((1,), (1,)), ((), ())), preferred_element_type=f32)


def iota(shape, dim):
    return lax.broadcasted_iota(jnp.int32, shape, dim)


def rms(values, gain):
    mean = jnp.mean(values * values, axis=-1, keepdims=True)
    return values * lax.rsqrt(mean + 1e-05) * gain


def pack_kernel(band_ref, count_ref, flags_ref, x_ref, work_ref, give_ref, south_ref, north_ref, west_ref, east_ref):
    variables, levels, rows, cols = x_ref.shape
    pairs = variables * levels
    live = (flags_ref[...] == 1) & (iota((rows, cols), 0) < count_ref[0, 0])
    live = jnp.where(live, 1.0, 0.0)
    extra = work_ref.shape[0] - pairs
    west, east = [], []
    for y in range(rows):
        here = slice(y * cols, (y + 1) * cols)
        state = x_ref[:, :, y, :].reshape(pairs, cols)
        work_ref[:pairs, here] = state.astype(bf16)
        work_ref[pairs:, here] = jnp.where(
            iota((extra, cols), 0) == 0, live[y : y + 1, :], 0.0
        ).astype(bf16)
        west.append(state[:, :1])
        east.append(state[:, cols - 1 :])
    give_ref[...] = work_ref[:, rows * cols - give_ref.shape[1] :]
    first, last = work_ref[:pairs, :cols], work_ref[:pairs, (rows - 1) * cols :]
    if south_ref is None:
        north_ref[...] = jnp.where(band_ref[0, 0] == 0, last, first)
    else:
        north_ref[...] = last
        south_ref[...] = first
    lane = iota((pairs, LANES), 1)
    for ref, edges in ((west_ref, west), (east_ref, east)):
        total = jnp.zeros((pairs, LANES), f32)
        for y in range(rows):
            total = jnp.where(lane == y, edges[y], total)
        ref[...] = total.astype(bf16)


def network_kernel(
    phase,
    work_ref,
    got_ref,
    embed_ref,
    level_ref,
    gains_ref,
    qkv_ref,
    out_w_ref,
    up_ref,
    down_ref,
    head_ref,
    phys_ref,
    inputs_sc,
    table_sc,
    pos_sc,
    heads_sc,
):
    variables = embed_ref.shape[0]
    levels = level_ref.shape[0]
    width = out_w_ref.shape[0]
    cols = phys_ref.shape[1]
    given = got_ref.shape[1]
    head_size = width // HEADS
    pairs = variables * levels
    depth = inputs_sc.shape[0]
    tokens = levels * CHAIN
    group_tokens = levels * GROUP
    zero = jnp.zeros((), bf16)

    mask_rows = work_ref.shape[0] - pairs
    helping = jnp.max(got_ref[pairs:, :].astype(f32)) > 0.5

    def take(source, start):
        inputs_sc[:pairs, :] = source[:pairs, start : start + cols]
        pos_sc[...] = source[pairs : pairs + mask_rows, start : start + cols].astype(f32)

    if phase == 0:
        pl.when(helping)(lambda: take(got_ref, 0))
        pl.when(jnp.logical_not(helping))(lambda: take(work_ref, 0))
    else:
        pl.when(helping)(lambda: take(work_ref, 0))
        pl.when(jnp.logical_not(helping))(lambda: take(work_ref, given))
    inputs_sc[pairs:, :] = jnp.where(
        iota((depth - pairs, cols), 0) < levels, 1.0, 0.0
    ).astype(bf16)

    live = pos_sc[...]
    before = jnp.where(iota((cols, cols), 0) < iota((cols, cols), 1), 1.0, 0.0).astype(bf16)
    place = dot(live.astype(bf16), before)
    pos_sc[...] = jnp.where(live > 0.5, place, -1.0)
    total_live = jnp.sum(live).astype(jnp.int32)
    phys_ref[...] = jnp.zeros(phys_ref.shape, phys_ref.dtype)
    for f in range(variables):
        table_sc[f * levels : (f + 1) * levels, :] = jnp.broadcast_to(
            embed_ref[f : f + 1, :].astype(f32), (levels, width)
        ).astype(bf16)
    table_sc[pairs : pairs + levels, :] = level_ref[...]
    table_sc[pairs + levels :, :] = jnp.zeros((depth - pairs - levels, width), bf16)
    block_diag = iota((width, width), 0) // head_size == iota((width, width), 1) // head_size
    heads_sc[...] = jnp.where(block_diag, 1.0 / head_size, 0.0).astype(bf16)

    def embed(packed):
        lane_level = iota((levels, depth), 1) % levels
        parts = []
        for g in range(CHAIN // GROUP):
            rows_g = packed[g * GROUP : (g + 1) * GROUP, :]
            for l in range(levels):
                parts.append(jnp.where(lane_level == l, rows_g, 0.0))
        return dot(jnp.concatenate(parts, axis=0).astype(bf16), table_sc[...])

    def project(hidden):
        normed = rms(hidden, gains_ref[0:1, :]).astype(bf16)
        queries = dot(normed, qkv_ref[:, :width])
        keys = dot(normed, qkv_ref[:, width : 2 * width])
        values = dot(normed, qkv_ref[:, 2 * width :]).astype(bf16)
        return queries, keys, values

    def normalize(queries, keys):
        both = jnp.concatenate([queries, keys], axis=0)
        mean = dot((both * both).astype(bf16), heads_sc[...])
        q_mean, k_mean = mean[:tokens], mean[tokens:]
        queries = (queries * (lax.rsqrt(q_mean + 1e-05) * head_size**-0.5)).astype(bf16)
        keys = (keys * lax.rsqrt(k_mean + 1e-05)).astype(bf16)
        return queries, keys

    def split(part):
        head_of = iota((group_tokens, width), 1) // head_size
        return jnp.concatenate(
            [jnp.where(head_of == h, part, zero) for h in range(HEADS)], axis=0
        )

    def attend(parts):
        same = (iota((group_tokens, width), 0) % GROUP) == (iota((group_tokens, width), 1) % GROUP)
        groups = [
            (c, slice(g * group_tokens, (g + 1) * group_tokens))
            for c in range(len(parts))
            for g in range(CHAIN // GROUP)
        ]
        scores = [dot_nt(parts[c][0][h], split(parts[c][1][h])) for c, h in groups]
        probs = [jnp.where(same, jnp.exp(v), 0.0).astype(bf16) for v in scores]
        mixed = [dot(p, split(parts[c][2][h])) for p, (c, h) in zip(probs, groups)]
        total = dot(jnp.concatenate(probs, axis=0), heads_sc[...]) * head_size
        mixed = (jnp.concatenate(mixed, axis=0) / total).astype(bf16)
        return [mixed[c * tokens : (c + 1) * tokens] for c in range(len(parts))]

    def feed(after_attn):
        normed = (rms(after_attn, gains_ref[1:2, :]) * 0.5).astype(bf16)
        inner = dot(normed, up_ref[...])
        inner = (inner + inner * jnp.tanh(inner)).astype(bf16)
        return after_attn + dot(inner, down_ref[...])

    def finish(after_mlp):
        normed = rms(after_mlp, gains_ref[2:3, :]).astype(bf16)
        tend = dot_nt(head_ref[...], normed)
        level_of = (iota((levels, tokens), 1) // GROUP) % levels == iota((levels, tokens), 0)
        return jnp.concatenate(
            [
                jnp.where(level_of, jnp.broadcast_to(tend[f : f + 1, :], (levels, tokens)), 0.0)
                for f in range(variables)
            ],
            axis=0,
        ).astype(bf16)

    def evaluate(start, chains):
        slots = (iota((chains * CHAIN, cols), 0) + start).astype(f32)
        pick = jnp.where(pos_sc[0:1, :] == slots, 1.0, 0.0)
        packed = dot_nt(pick.astype(bf16), inputs_sc[...])
        span = range(chains)
        hidden = [embed(packed[i * CHAIN : (i + 1) * CHAIN, :]) for i in span]
        qkv = [project(h) for h in hidden]
        qk = [normalize(q, k) for q, k, _ in qkv]
        mixed = attend([(*qk[i], qkv[i][2]) for i in span])
        after = [hidden[i] + dot(mixed[i], out_w_ref[...]) for i in span]
        after = [feed(a) for a in after]
        placed = jnp.concatenate([finish(a) for a in after], axis=1)
        parts = []
        for g in range(chains * CHAIN // GROUP):
            part = pick[g * GROUP : (g + 1) * GROUP, :]
            part = jnp.concatenate([part, part], axis=0).astype(bf16)
            parts.extend([part] * (levels // 2))
        phys_ref[...] += dot(placed, jnp.concatenate(parts, axis=0)).astype(phys_ref.dtype)

    units = (total_live + (CHAIN - 1)) // CHAIN
    rounds = units // CHAINS

    def body(t, carry):
        evaluate(t * (CHAIN * CHAINS), CHAINS)
        return carry

    lax.fori_loop(0, rounds, body, 0)
    rest = units - rounds * CHAINS
    for chains in range(1, CHAINS):
        pl.when(rest == chains)(
            functools.partial(evaluate, rounds * (CHAIN * CHAINS), chains)
        )


def final_kernel(
    band_ref, bands, x_ref, diffusion_ref, work_ref, got_ref, a_ref, b_ref, back_ref,
    south_ref, north_ref, west_ref, east_ref, out_ref, phys_sc,
):
    variables, levels, rows, cols = x_ref.shape
    pairs = variables * levels
    whole = rows * cols
    na, nb = a_ref.shape[1], b_ref.shape[1]
    helping = jnp.max(got_ref[pairs:, :].astype(f32)) > 0.5

    @pl.when(helping)
    def _():
        phys_sc[:, :nb] = b_ref[...]
        phys_sc[:, nb:] = jnp.zeros((pairs, whole - nb), phys_sc.dtype)

    @pl.when(jnp.logical_not(helping))
    def _():
        phys_sc[:, :na] = a_ref[...]
        phys_sc[:, na : na + nb] = b_ref[...]
        phys_sc[:, na + nb :] = back_ref[...]

    level = iota((levels, levels), 0) == iota((levels, levels), 1)
    rate = jnp.concatenate(
        [
            jnp.sum(
                jnp.where(level, jnp.broadcast_to(diffusion_ref[f : f + 1, :], (levels, levels)), 0.0),
                axis=1,
                keepdims=True,
            )
            for f in range(variables)
        ],
        axis=0,
    )
    state = [x_ref[:, :, y, :].reshape(pairs, cols) for y in range(rows)]
    band = band_ref[0, 0]
    above = jnp.where(band > 0, north_ref[...].astype(f32), 0.0)
    below = jnp.where(band < bands - 1, south_ref[...].astype(f32), 0.0)
    lane = iota((pairs, cols), 1)
    for y in range(rows):
        here = state[y]
        left = jnp.where(lane == 0, west_ref[:, y : y + 1].astype(f32), pltpu.roll(here, 1, 1))
        right = jnp.where(
            lane == cols - 1, east_ref[:, y : y + 1].astype(f32), pltpu.roll(here, cols - 1, 1)
        )
        up = state[y - 1] if y > 0 else above
        down = state[y + 1] if y < rows - 1 else below
        laplace = left + right + up + down - 4.0 * here
        span = slice(y * cols, (y + 1) * cols)
        live = work_ref[pairs : pairs + 1, span].astype(f32) > 0.5
        tend = jnp.where(live, phys_sc[:, span].astype(f32), 0.0)
        out_ref[:, :, y, :] = (here + rate * laplace + tend).reshape(variables, levels, cols)


VMEM = pl.BlockSpec(memory_space=pltpu.VMEM)
SMEM = pl.BlockSpec(memory_space=pltpu.SMEM)


def shape(dims, dtype=bf16):
    return jax.ShapeDtypeStruct(dims, dtype)


def network(phase, cols, work, got, weights, dims):
    variables, levels = dims
    w_embed, level_embed, norm_gains, w_qkv, w_out, w_up, w_down, head_t = weights
    width = w_out.shape[0]
    pairs = variables * levels
    depth = -(-(pairs + levels) // 64) * 64
    return pl.pallas_call(
        functools.partial(network_kernel, phase),
        out_shape=shape((pairs, cols)),
        in_specs=[VMEM] * 10,
        out_specs=VMEM,
        scratch_shapes=[
            pltpu.VMEM((depth, cols), bf16),
            pltpu.VMEM((depth, width), bf16),
            pltpu.VMEM((work.shape[0] - pairs, cols), f32),
            pltpu.VMEM((width, width), bf16),
        ],
        compiler_params=pltpu.CompilerParams(vmem_limit_bytes=16 << 20),
        cost_estimate=pl.CostEstimate(
            flops=3_000_000_000, bytes_accessed=2_000_000, transcendentals=4_000_000
        ),
        name="column_physics",
    )(work, got, w_embed, level_embed, norm_gains, w_qkv, w_out, w_up, w_down, head_t)


def load_kernel(after_ref, *refs):
    count = len(refs) // 2
    sems = refs[-1]
    copies = [
        pltpu.make_async_copy(refs[i], refs[count + i], sems.at[i]) for i in range(count)
    ]
    for copy in copies:
        copy.start()
    for copy in copies:
        copy.wait()


def load(after, arrays):
    hbm = pl.BlockSpec(memory_space=pltpu.HBM)
    return pl.pallas_call(
        load_kernel,
        out_shape=[shape(w.shape, w.dtype) for w in arrays],
        in_specs=[VMEM] + [hbm] * len(arrays),
        out_specs=[VMEM] * len(arrays),
        scratch_shapes=[pltpu.SemaphoreType.DMA((len(arrays),))],
        compiler_params=pltpu.CompilerParams(vmem_limit_bytes=8 << 20),
        cost_estimate=pl.CostEstimate(flops=0, bytes_accessed=4_000_000, transcendentals=0),
        name="load_weights",
    )(after, *(pltpu.with_memory_space_constraint(w, pltpu.HBM) for w in arrays))


def pack(band, block_counts, conv_flags, column_state, given, two_bands):
    variables, levels, rows, cols = column_state.shape
    pairs = variables * levels
    tall = pairs + 8
    row = shape((pairs, cols))
    edge = shape((pairs, LANES))
    outs = [shape((tall, rows * cols)), shape((tall, given))]
    outs += [row] if two_bands else [row, row]
    outs += [edge, edge]

    def kernel(*refs):
        if two_bands:
            refs = refs[:6] + (None,) + refs[6:]
        pack_kernel(*refs)

    return pl.pallas_call(
        kernel,
        out_shape=outs,
        in_specs=[SMEM, SMEM, VMEM, VMEM],
        out_specs=[VMEM] * len(outs),
        compiler_params=pltpu.CompilerParams(vmem_limit_bytes=8 << 20),
        name="pack",
    )(band, block_counts, conv_flags, column_state)


def physics(block_counts, conv_flags, column_state, weights):
    weights = weights[:-1] + (weights[-1].T,)
    band = jnp.zeros((1, 1), jnp.int32)
    work, give, *_ = pack(band, block_counts, conv_flags, column_state, 384, True)
    got = jnp.zeros_like(give)
    a = network(0, 384, work, got, weights, (6, 8))
    return a


def shards(column_state, conv_flags, block_counts, diffusion, *weights):
    variables, levels, rows, cols = column_state.shape
    pairs = variables * levels
    weights = weights[:-1] + (weights[-1].T,)
    tiles, bands = lax.axis_size("tile"), lax.axis_size("band")
    given = cols + cols // 2
    kept = rows * cols - 2 * given
    band = lax.axis_index("band").reshape(1, 1).astype(jnp.int32)
    packed = pack(band, block_counts, conv_flags, column_state, given, bands == 2)
    work, give = packed[:2]
    pairing = [(i, i ^ 1) for i in range(tiles)]
    got = lax.ppermute(give, "tile", pairing)
    if bands == 2:
        north = south = lax.ppermute(packed[2], "band", [(0, 1), (1, 0)])
    else:
        south = lax.ppermute(packed[2], "band", [(i + 1, i) for i in range(bands - 1)])
        north = lax.ppermute(packed[3], "band", [(i, i + 1) for i in range(bands - 1)])
    forward = [(i, (i + 1) % tiles) for i in range(tiles)]
    backward = [((i + 1) % tiles, i) for i in range(tiles)]
    east = lax.ppermute(packed[-2], "tile", backward)
    west = lax.ppermute(packed[-1], "tile", forward)
    weights = (*weights[:3], *load(packed[-1], weights[3:7]), weights[7])
    a = network(0, given, work, got, weights, (variables, levels))
    back = lax.ppermute(a, "tile", pairing)
    b = network(1, kept, work, got, weights, (variables, levels))

    def kernel(band_ref, *refs):
        final_kernel(band_ref, bands, *refs)

    return pl.pallas_call(
        kernel,
        out_shape=shape(column_state.shape, f32),
        in_specs=[SMEM] + [VMEM] * 11,
        out_specs=VMEM,
        scratch_shapes=[pltpu.VMEM((pairs, rows * cols), bf16)],
        compiler_params=pltpu.CompilerParams(vmem_limit_bytes=8 << 20),
        name="combine",
    )(band, column_state, diffusion, work, got, a, b, back, south, north, west, east)


def solution(mesh):
    placed = (
        P(None, None, "band", "tile"),
        P("band", "tile"),
        P("band", "tile"),
        P(),
        P(),
        P(),
        P(),
        P(),
        P(),
        P(),
        P(),
        P(),
    )
    return jax.shard_map(
        shards, mesh=mesh, in_specs=placed, out_specs=P(None, None, "band", "tile"), check_vma=False
    )
```

```python
import functools

import jax
import jax.numpy as jnp
from jax import lax
from jax.experimental import pallas as pl
from jax.experimental.pallas import tpu as pltpu
from jax.sharding import PartitionSpec as P

HEADS = 4
CHAIN = 32
CHAINS = 6
GROUP = 8
LANES = 128
bf16 = jnp.bfloat16
f32 = jnp.float32


def dot(a, b):
    return jnp.dot(a, b, preferred_element_type=f32)


def dot_nt(a, b):
    return lax.dot_general(a, b, (((1,), (1,)), ((), ())), preferred_element_type=f32)


def iota(shape, dim):
    return lax.broadcasted_iota(jnp.int32, shape, dim)


def rms(values, gain):
    mean = jnp.mean(values * values, axis=-1, keepdims=True)
    return values * lax.rsqrt(mean + 1e-05) * gain


def pack_kernel(band_ref, count_ref, flags_ref, x_ref, work_ref, give_ref, south_ref, north_ref, west_ref, east_ref):
    variables, levels, rows, cols = x_ref.shape
    pairs = variables * levels
    live = (flags_ref[...] == 1) & (iota((rows, cols), 0) < count_ref[0, 0])
    live = jnp.where(live, 1.0, 0.0)
    extra = work_ref.shape[0] - pairs
    west, east = [], []
    for y in range(rows):
        here = slice(y * cols, (y + 1) * cols)
        state = x_ref[:, :, y, :].reshape(pairs, cols)
        work_ref[:pairs, here] = state.astype(bf16)
        work_ref[pairs:, here] = jnp.where(
            iota((extra, cols), 0) == 0, live[y : y + 1, :], 0.0
        ).astype(bf16)
        west.append(state[:, :1])
        east.append(state[:, cols - 1 :])
    give_ref[...] = work_ref[:, rows * cols - give_ref.shape[1] :]
    first, last = work_ref[:pairs, :cols], work_ref[:pairs, (rows - 1) * cols :]
    if south_ref is None:
        north_ref[...] = jnp.where(band_ref[0, 0] == 0, last, first)
    else:
        north_ref[...] = last
        south_ref[...] = first
    lane = iota((pairs, LANES), 1)
    for ref, edges in ((west_ref, west), (east_ref, east)):
        total = jnp.zeros((pairs, LANES), f32)
        for y in range(rows):
            total = jnp.where(lane == y, edges[y], total)
        ref[...] = total.astype(bf16)


def network_kernel(
    phase,
    dims,
    work_ref,
    got_ref,
    table_sc,
    heads_sc,
    gains_ref,
    qkv_ref,
    out_w_ref,
    up_ref,
    down_ref,
    head_ref,
    phys_ref,
    inputs_sc,
    pos_sc,
):
    variables, levels = dims
    width = out_w_ref.shape[0]
    cols = phys_ref.shape[1]
    given = got_ref.shape[1]
    head_size = width // HEADS
    pairs = variables * levels
    depth = inputs_sc.shape[0]
    tokens = levels * CHAIN
    group_tokens = levels * GROUP
    zero = jnp.zeros((), bf16)

    before = jnp.where(iota((cols, cols), 0) < iota((cols, cols), 1), 1.0, 0.0).astype(bf16)
    inputs_sc[pairs:, :] = jnp.where(
        iota((depth - pairs, cols), 0) < levels, 1.0, 0.0
    ).astype(bf16)

    def sum_of(source, start):
        return jnp.sum(source[pairs:, start : start + cols].astype(f32)).astype(jnp.int32)

    helped = jnp.sum(got_ref[pairs:, :].astype(f32)).astype(jnp.int32)
    helping = helped > 0
    if phase == 0:
        choices = ((got_ref, 0), (work_ref, 0))
        total_live = jnp.where(helping, helped, sum_of(work_ref, 0))
    else:
        choices = ((work_ref, 0), (work_ref, given))
        total_live = jnp.where(helping, sum_of(work_ref, 0), sum_of(work_ref, given))

    def take(source, start):
        inputs_sc[:pairs, :] = source[:pairs, start : start + cols]
        pos_sc[...] = source[pairs:, start : start + cols].astype(f32)

    pl.when(helping)(functools.partial(take, *choices[0]))
    pl.when(jnp.logical_not(helping))(functools.partial(take, *choices[1]))
    live = pos_sc[...]
    place = dot(live.astype(bf16), before)
    pos_sc[...] = jnp.where(live > 0.5, place, -1.0)
    phys_ref[...] = jnp.zeros(phys_ref.shape, phys_ref.dtype)
    def embed(packed):
        lane_level = iota((levels, depth), 1) % levels
        parts = []
        for g in range(CHAIN // GROUP):
            rows_g = packed[g * GROUP : (g + 1) * GROUP, :]
            for l in range(levels):
                parts.append(jnp.where(lane_level == l, rows_g, 0.0))
        return dot(jnp.concatenate(parts, axis=0).astype(bf16), table_sc[...])

    def project(hidden):
        normed = rms(hidden, gains_ref[0:1, :]).astype(bf16)
        queries = dot(normed, qkv_ref[:, :width])
        keys = dot(normed, qkv_ref[:, width : 2 * width])
        values = dot(normed, qkv_ref[:, 2 * width :]).astype(bf16)
        return queries, keys, values

    def normalize(queries, keys):
        both = jnp.concatenate([queries, keys], axis=0)
        mean = dot((both * both).astype(bf16), heads_sc[...])
        q_mean, k_mean = mean[:tokens], mean[tokens:]
        queries = (queries * (lax.rsqrt(q_mean + 1e-05) * head_size**-0.5)).astype(bf16)
        keys = (keys * lax.rsqrt(k_mean + 1e-05)).astype(bf16)
        return queries, keys

    def split(part):
        head_of = iota((group_tokens, width), 1) // head_size
        return jnp.concatenate(
            [jnp.where(head_of == h, part, zero) for h in range(HEADS)], axis=0
        )

    def attend(parts):
        same = (iota((group_tokens, width), 0) % GROUP) == (iota((group_tokens, width), 1) % GROUP)
        groups = [
            (c, slice(g * group_tokens, (g + 1) * group_tokens))
            for c in range(len(parts))
            for g in range(CHAIN // GROUP)
        ]
        scores = [dot_nt(parts[c][0][h], split(parts[c][1][h])) for c, h in groups]
        probs = [jnp.where(same, jnp.exp(v), 0.0).astype(bf16) for v in scores]
        mixed = [dot(p, split(parts[c][2][h])) for p, (c, h) in zip(probs, groups)]
        total = dot(jnp.concatenate(probs, axis=0), heads_sc[...]) * head_size
        mixed = (jnp.concatenate(mixed, axis=0) / total).astype(bf16)
        return [mixed[c * tokens : (c + 1) * tokens] for c in range(len(parts))]

    def feed(after_attn):
        normed = (rms(after_attn, gains_ref[1:2, :]) * 0.5).astype(bf16)
        inner = dot(normed, up_ref[...])
        inner = (inner + inner * jnp.tanh(inner)).astype(bf16)
        return after_attn + dot(inner, down_ref[...])

    def finish(after_mlp):
        normed = rms(after_mlp, gains_ref[2:3, :]).astype(bf16)
        tend = dot_nt(head_ref[...], normed)
        level_of = (iota((levels, tokens), 1) // GROUP) % levels == iota((levels, tokens), 0)
        return jnp.concatenate(
            [
                jnp.where(level_of, jnp.broadcast_to(tend[f : f + 1, :], (levels, tokens)), 0.0)
                for f in range(variables)
            ],
            axis=0,
        ).astype(bf16)

    def evaluate(start, chains):
        slots = (iota((chains * CHAIN, cols), 0) + start).astype(f32)
        pick = jnp.where(pos_sc[0:1, :] == slots, 1.0, 0.0)
        packed = dot_nt(pick.astype(bf16), inputs_sc[...])
        span = range(chains)
        hidden = [embed(packed[i * CHAIN : (i + 1) * CHAIN, :]) for i in span]
        qkv = [project(h) for h in hidden]
        qk = [normalize(q, k) for q, k, _ in qkv]
        mixed = attend([(*qk[i], qkv[i][2]) for i in span])
        after = [hidden[i] + dot(mixed[i], out_w_ref[...]) for i in span]
        after = [feed(a) for a in after]
        placed = jnp.concatenate([finish(a) for a in after], axis=1)
        parts = []
        for g in range(chains * CHAIN // GROUP):
            part = pick[g * GROUP : (g + 1) * GROUP, :]
            part = jnp.concatenate([part, part], axis=0).astype(bf16)
            parts.extend([part] * (levels // 2))
        phys_ref[...] += dot(placed, jnp.concatenate(parts, axis=0)).astype(phys_ref.dtype)

    units = (total_live + (CHAIN - 1)) // CHAIN
    rounds = (units + 1) // CHAINS

    def body(t, carry):
        evaluate(t * (CHAIN * CHAINS), CHAINS)
        return carry

    lax.fori_loop(0, rounds, body, 0)
    rest = units - rounds * CHAINS
    for chains in range(2, CHAINS - 1, 2):
        pl.when((rest == chains) | (rest == chains - 1))(
            functools.partial(evaluate, rounds * (CHAIN * CHAINS), chains)
        )


def final_kernel(
    band_ref, bands, x_ref, diffusion_ref, work_ref, got_ref, a_ref, b_ref, back_ref,
    south_ref, north_ref, west_ref, east_ref, out_ref, phys_sc,
):
    variables, levels, rows, cols = x_ref.shape
    pairs = variables * levels
    whole = rows * cols
    na, nb = a_ref.shape[1], b_ref.shape[1]
    helping = jnp.max(got_ref[pairs:, :].astype(f32)) > 0.5

    @pl.when(helping)
    def _():
        phys_sc[:, :nb] = b_ref[...]
        phys_sc[:, nb:] = jnp.zeros((pairs, whole - nb), phys_sc.dtype)

    @pl.when(jnp.logical_not(helping))
    def _():
        phys_sc[:, :na] = a_ref[...]
        phys_sc[:, na : na + nb] = b_ref[...]
        phys_sc[:, na + nb :] = back_ref[...]

    level = iota((levels, levels), 0) == iota((levels, levels), 1)
    rate = jnp.concatenate(
        [
            jnp.sum(
                jnp.where(level, jnp.broadcast_to(diffusion_ref[f : f + 1, :], (levels, levels)), 0.0),
                axis=1,
                keepdims=True,
            )
            for f in range(variables)
        ],
        axis=0,
    )
    state = [x_ref[:, :, y, :].reshape(pairs, cols) for y in range(rows)]
    band = band_ref[0, 0]
    above = jnp.where(band > 0, north_ref[...].astype(f32), 0.0)
    below = jnp.where(band < bands - 1, south_ref[...].astype(f32), 0.0)
    lane = iota((pairs, cols), 1)
    for y in range(rows):
        here = state[y]
        left = jnp.where(lane == 0, west_ref[:, y : y + 1].astype(f32), pltpu.roll(here, 1, 1))
        right = jnp.where(
            lane == cols - 1, east_ref[:, y : y + 1].astype(f32), pltpu.roll(here, cols - 1, 1)
        )
        up = state[y - 1] if y > 0 else above
        down = state[y + 1] if y < rows - 1 else below
        laplace = left + right + up + down - 4.0 * here
        span = slice(y * cols, (y + 1) * cols)
        live = work_ref[pairs : pairs + 1, span].astype(f32) > 0.5
        tend = jnp.where(live, phys_sc[:, span].astype(f32), 0.0)
        out_ref[:, :, y, :] = (here + rate * laplace + tend).reshape(variables, levels, cols)


VMEM = pl.BlockSpec(memory_space=pltpu.VMEM)
SMEM = pl.BlockSpec(memory_space=pltpu.SMEM)


def shape(dims, dtype=bf16):
    return jax.ShapeDtypeStruct(dims, dtype)


def network(phase, cols, work, got, weights, dims):
    variables, levels = dims
    table, heads, norm_gains, w_qkv, w_out, w_up, w_down, head_t = weights
    pairs = variables * levels
    depth = table.shape[0]
    return pl.pallas_call(
        functools.partial(network_kernel, phase, dims),
        out_shape=shape((pairs, cols)),
        in_specs=[VMEM] * 10,
        out_specs=VMEM,
        scratch_shapes=[
            pltpu.VMEM((depth, cols), bf16),
            pltpu.VMEM((work.shape[0] - pairs, cols), f32),
        ],
        compiler_params=pltpu.CompilerParams(vmem_limit_bytes=16 << 20),
        cost_estimate=pl.CostEstimate(
            flops=3_000_000_000, bytes_accessed=2_000_000, transcendentals=4_000_000
        ),
        name="column_physics",
    )(work, got, table, heads, norm_gains, w_qkv, w_out, w_up, w_down, head_t)


def load_kernel(after_ref, embed_ref, level_ref, *refs):
    count = (len(refs) - 3) // 2
    sems = refs[-1]
    table_ref, heads_ref = refs[2 * count : 2 * count + 2]
    copies = [
        pltpu.make_async_copy(refs[i], refs[count + i], sems.at[i]) for i in range(count)
    ]
    for copy in copies:
        copy.start()
    variables, levels = embed_ref.shape[0], level_ref.shape[0]
    depth, width = table_ref.shape
    pairs = variables * levels
    head_size = width // HEADS
    for f in range(variables):
        table_ref[f * levels : (f + 1) * levels, :] = jnp.broadcast_to(
            embed_ref[f : f + 1, :].astype(f32), (levels, width)
        ).astype(bf16)
    table_ref[pairs : pairs + levels, :] = level_ref[...]
    table_ref[pairs + levels :, :] = jnp.zeros((depth - pairs - levels, width), bf16)
    same = iota((width, width), 0) // head_size == iota((width, width), 1) // head_size
    heads_ref[...] = jnp.where(same, 1.0 / head_size, 0.0).astype(bf16)
    for copy in copies:
        copy.wait()


def load(after, w_embed, level_embed, *arrays):
    hbm = pl.BlockSpec(memory_space=pltpu.HBM)
    variables, width = w_embed.shape
    levels = level_embed.shape[0]
    depth = -(-(variables + 1) * levels // 64) * 64
    outs = [shape(w.shape, w.dtype) for w in arrays]
    outs += [shape((depth, width)), shape((width, width))]
    *loaded, table, heads = pl.pallas_call(
        load_kernel,
        out_shape=outs,
        in_specs=[VMEM] * 3 + [hbm] * len(arrays),
        out_specs=[VMEM] * len(outs),
        scratch_shapes=[pltpu.SemaphoreType.DMA((len(arrays),))],
        compiler_params=pltpu.CompilerParams(vmem_limit_bytes=8 << 20),
        cost_estimate=pl.CostEstimate(flops=0, bytes_accessed=4_000_000, transcendentals=0),
        name="load_weights",
    )(
        after,
        w_embed,
        level_embed,
        *(pltpu.with_memory_space_constraint(w, pltpu.HBM) for w in arrays),
    )
    return table, heads, *loaded


def pack(band, block_counts, conv_flags, column_state, given, two_bands):
    variables, levels, rows, cols = column_state.shape
    pairs = variables * levels
    tall = pairs + 8
    row = shape((pairs, cols))
    edge = shape((pairs, LANES))
    outs = [shape((tall, rows * cols)), shape((tall, given))]
    outs += [row] if two_bands else [row, row]
    outs += [edge, edge]

    def kernel(*refs):
        if two_bands:
            refs = refs[:6] + (None,) + refs[6:]
        pack_kernel(*refs)

    return pl.pallas_call(
        kernel,
        out_shape=outs,
        in_specs=[SMEM, SMEM, VMEM, VMEM],
        out_specs=[VMEM] * len(outs),
        compiler_params=pltpu.CompilerParams(vmem_limit_bytes=8 << 20),
        name="pack",
    )(band, block_counts, conv_flags, column_state)


def shards(column_state, conv_flags, block_counts, diffusion, *weights):
    variables, levels, rows, cols = column_state.shape
    pairs = variables * levels
    weights = weights[:-1] + (weights[-1].T,)
    tiles, bands = lax.axis_size("tile"), lax.axis_size("band")
    given = cols + 3 * cols // 8
    kept = rows * cols - 2 * given
    band = lax.axis_index("band").reshape(1, 1).astype(jnp.int32)
    packed = pack(band, block_counts, conv_flags, column_state, given, bands == 2)
    work, give = packed[:2]
    pairing = [(i, i ^ 1) for i in range(tiles)]
    forward = [(i, (i + 1) % tiles) for i in range(tiles)]
    backward = [((i + 1) % tiles, i) for i in range(tiles)]
    got = lax.ppermute(give, "tile", pairing)
    weights = load(packed[-1], *weights)
    a = network(0, given, work, got, weights, (variables, levels))
    a, *edges = lax.optimization_barrier((a, *packed[2:]))
    back = lax.ppermute(a, "tile", pairing)
    if bands == 2:
        north = south = lax.ppermute(edges[0], "band", [(0, 1), (1, 0)])
    else:
        south = lax.ppermute(edges[0], "band", [(i + 1, i) for i in range(bands - 1)])
        north = lax.ppermute(edges[1], "band", [(i, i + 1) for i in range(bands - 1)])
    east = lax.ppermute(edges[-2], "tile", backward)
    west = lax.ppermute(edges[-1], "tile", forward)
    b = network(1, kept, work, got, weights, (variables, levels))

    def kernel(band_ref, *refs):
        final_kernel(band_ref, bands, *refs)

    return pl.pallas_call(
        kernel,
        out_shape=shape(column_state.shape, f32),
        in_specs=[SMEM] + [VMEM] * 11,
        out_specs=VMEM,
        scratch_shapes=[pltpu.VMEM((pairs, rows * cols), bf16)],
        compiler_params=pltpu.CompilerParams(vmem_limit_bytes=8 << 20),
        name="combine",
    )(band, column_state, diffusion, work, got, a, b, back, south, north, west, east)


def solution(mesh):
    placed = (
        P(None, None, "band", "tile"),
        P("band", "tile"),
        P("band", "tile"),
        P(),
        P(),
        P(),
        P(),
        P(),
        P(),
        P(),
        P(),
        P(),
    )
    return jax.shard_map(
        shards, mesh=mesh, in_specs=placed, out_specs=P(None, None, "band", "tile"), check_vma=False
    )
```

```python
import functools

import jax
import jax.numpy as jnp
from jax import lax
from jax.experimental import pallas as pl
from jax.experimental.pallas import tpu as pltpu
from jax.sharding import PartitionSpec as P

HEADS = 4
CHAIN = 32
CHAINS = 6
GROUP = 8
LANES = 128
bf16 = jnp.bfloat16
f32 = jnp.float32


def dot(a, b):
    return jnp.dot(a, b, preferred_element_type=f32)


def dot_nt(a, b):
    return lax.dot_general(a, b, (((1,), (1,)), ((), ())), preferred_element_type=f32)


def iota(shape, dim):
    return lax.broadcasted_iota(jnp.int32, shape, dim)


def rms(values, gain):
    mean = jnp.mean(values * values, axis=-1, keepdims=True)
    return values * lax.rsqrt(mean + 1e-05) * gain


def pack_kernel(
    given, place_ref, count_ref, flags_ref, x_ref, work_ref, give_ref, south_ref, north_ref, swap_ref
):
    variables, levels, rows, cols = x_ref.shape
    pairs = variables * levels
    live = (flags_ref[...] == 1) & (iota((rows, cols), 0) < count_ref[0, 0])
    live = jnp.where(live, 1.0, 0.0)
    extra = work_ref.shape[0] - pairs
    west, east = [], []
    for y in range(rows):
        here = slice(y * cols, (y + 1) * cols)
        state = x_ref[:, :, y, :].reshape(pairs, cols)
        work_ref[:pairs, here] = state.astype(bf16)
        work_ref[pairs:, here] = jnp.where(
            iota((extra, cols), 0) == 0, live[y : y + 1, :], 0.0
        ).astype(bf16)
        west.append(state[:, :1])
        east.append(state[:, cols - 1 :])
    first, last = work_ref[:pairs, :cols], work_ref[:pairs, (rows - 1) * cols :]
    if south_ref is None:
        north_ref[...] = jnp.where(place_ref[0] == 0, last, first)
    else:
        north_ref[...] = last
        south_ref[...] = first
    even = place_ref[1] % 2 == 0
    lane = iota((pairs, LANES), 1)
    outer = jnp.zeros((pairs, LANES), f32)
    inner = jnp.zeros((pairs, LANES), f32)
    shift = given % LANES
    for y in range(rows):
        outer = jnp.where(lane == y, jnp.where(even, west[y], east[y]), outer)
        inner = jnp.where(lane == shift + y, jnp.where(even, east[y], west[y]), inner)
    swap_ref[...] = outer.astype(bf16)
    whole = rows * cols
    give_ref[:, :given] = work_ref[:, whole - given :]
    tail = given - shift
    mixed = jnp.where(lane < shift, give_ref[:pairs, tail:].astype(f32), inner)
    give_ref[:pairs, tail:] = mixed.astype(bf16)
    extra_lane = iota((extra, LANES), 1)
    mask = jnp.where(extra_lane < shift, give_ref[pairs:, tail:].astype(f32), 0.0)
    give_ref[pairs:, tail:] = mask.astype(bf16)


def network_kernel(
    phase,
    dims,
    given,
    work_ref,
    got_ref,
    table_sc,
    heads_sc,
    gains_ref,
    qkv_ref,
    out_w_ref,
    up_ref,
    down_ref,
    head_ref,
    phys_ref,
    inputs_sc,
    pos_sc,
):
    variables, levels = dims
    width = out_w_ref.shape[0]
    cols = phys_ref.shape[1]
    head_size = width // HEADS
    pairs = variables * levels
    depth = inputs_sc.shape[0]
    tokens = levels * CHAIN
    group_tokens = levels * GROUP
    zero = jnp.zeros((), bf16)

    before = jnp.where(iota((cols, cols), 0) < iota((cols, cols), 1), 1.0, 0.0).astype(bf16)
    inputs_sc[pairs:, :] = jnp.where(
        iota((depth - pairs, cols), 0) < levels, 1.0, 0.0
    ).astype(bf16)

    def sum_of(source, start):
        return jnp.sum(source[pairs:, start : start + cols].astype(f32)).astype(jnp.int32)

    helped = jnp.sum(got_ref[pairs:, :].astype(f32)).astype(jnp.int32)
    helping = helped > 0
    if phase == 0:
        choices = ((got_ref, 0), (work_ref, 0))
        total_live = jnp.where(helping, helped, sum_of(work_ref, 0))
    else:
        choices = ((work_ref, 0), (work_ref, given))
        total_live = jnp.where(helping, sum_of(work_ref, 0), sum_of(work_ref, given))

    def take(source, start):
        inputs_sc[:pairs, :] = source[:pairs, start : start + cols]
        pos_sc[...] = source[pairs:, start : start + cols].astype(f32)

    pl.when(helping)(functools.partial(take, *choices[0]))
    pl.when(jnp.logical_not(helping))(functools.partial(take, *choices[1]))
    live = pos_sc[...]
    place = dot(live.astype(bf16), before)
    pos_sc[...] = jnp.where(live > 0.5, place, -1.0)
    phys_ref[...] = jnp.zeros(phys_ref.shape, phys_ref.dtype)
    def embed(packed):
        lane_level = iota((levels, depth), 1) % levels
        parts = []
        for g in range(CHAIN // GROUP):
            rows_g = packed[g * GROUP : (g + 1) * GROUP, :]
            for l in range(levels):
                parts.append(jnp.where(lane_level == l, rows_g, 0.0))
        return dot(jnp.concatenate(parts, axis=0).astype(bf16), table_sc[...])

    def project(hidden):
        normed = rms(hidden, gains_ref[0:1, :]).astype(bf16)
        queries = dot(normed, qkv_ref[:, :width])
        keys = dot(normed, qkv_ref[:, width : 2 * width])
        values = dot(normed, qkv_ref[:, 2 * width :]).astype(bf16)
        return queries, keys, values

    def normalize(queries, keys):
        both = jnp.concatenate([queries, keys], axis=0)
        mean = dot((both * both).astype(bf16), heads_sc[...])
        q_mean, k_mean = mean[:tokens], mean[tokens:]
        queries = (queries * (lax.rsqrt(q_mean + 1e-05) * head_size**-0.5)).astype(bf16)
        keys = (keys * lax.rsqrt(k_mean + 1e-05)).astype(bf16)
        return queries, keys

    def split(part):
        head_of = iota((group_tokens, width), 1) // head_size
        return jnp.concatenate(
            [jnp.where(head_of == h, part, zero) for h in range(HEADS)], axis=0
        )

    def attend(parts):
        same = (iota((group_tokens, width), 0) % GROUP) == (iota((group_tokens, width), 1) % GROUP)
        groups = [
            (c, slice(g * group_tokens, (g + 1) * group_tokens))
            for c in range(len(parts))
            for g in range(CHAIN // GROUP)
        ]
        scores = [dot_nt(parts[c][0][h], split(parts[c][1][h])) for c, h in groups]
        probs = [jnp.where(same, jnp.exp(v), 0.0).astype(bf16) for v in scores]
        mixed = [dot(p, split(parts[c][2][h])) for p, (c, h) in zip(probs, groups)]
        total = dot(jnp.concatenate(probs, axis=0), heads_sc[...]) * head_size
        mixed = (jnp.concatenate(mixed, axis=0) / total).astype(bf16)
        return [mixed[c * tokens : (c + 1) * tokens] for c in range(len(parts))]

    def feed(after_attn):
        normed = (rms(after_attn, gains_ref[1:2, :]) * 0.5).astype(bf16)
        inner = dot(normed, up_ref[...])
        inner = (inner + inner * jnp.tanh(inner)).astype(bf16)
        return after_attn + dot(inner, down_ref[...])

    def finish(after_mlp):
        normed = rms(after_mlp, gains_ref[2:3, :]).astype(bf16)
        tend = dot_nt(head_ref[...], normed)
        level_of = (iota((levels, tokens), 1) // GROUP) % levels == iota((levels, tokens), 0)
        return jnp.concatenate(
            [
                jnp.where(level_of, jnp.broadcast_to(tend[f : f + 1, :], (levels, tokens)), 0.0)
                for f in range(variables)
            ],
            axis=0,
        ).astype(bf16)

    def evaluate(start, chains):
        slots = (iota((chains * CHAIN, cols), 0) + start).astype(f32)
        pick = jnp.where(pos_sc[0:1, :] == slots, 1.0, 0.0)
        packed = dot_nt(pick.astype(bf16), inputs_sc[...])
        span = range(chains)
        hidden = [embed(packed[i * CHAIN : (i + 1) * CHAIN, :]) for i in span]
        qkv = [project(h) for h in hidden]
        qk = [normalize(q, k) for q, k, _ in qkv]
        mixed = attend([(*qk[i], qkv[i][2]) for i in span])
        after = [hidden[i] + dot(mixed[i], out_w_ref[...]) for i in span]
        after = [feed(a) for a in after]
        placed = jnp.concatenate([finish(a) for a in after], axis=1)
        parts = []
        for g in range(chains * CHAIN // GROUP):
            part = pick[g * GROUP : (g + 1) * GROUP, :]
            part = jnp.concatenate([part, part], axis=0).astype(bf16)
            parts.extend([part] * (levels // 2))
        phys_ref[...] += dot(placed, jnp.concatenate(parts, axis=0)).astype(phys_ref.dtype)

    units = (total_live + (CHAIN - 1)) // CHAIN
    rounds = (units + 1) // CHAINS

    def body(t, carry):
        evaluate(t * (CHAIN * CHAINS), CHAINS)
        return carry

    lax.fori_loop(0, rounds, body, 0)
    rest = units - rounds * CHAINS
    for chains in range(2, CHAINS - 1, 2):
        pl.when((rest == chains) | (rest == chains - 1))(
            functools.partial(evaluate, rounds * (CHAIN * CHAINS), chains)
        )


def final_kernel(
    place_ref, bands, x_ref, diffusion_ref, work_ref, got_ref, a_ref, b_ref, back_ref,
    south_ref, north_ref, swap_ref, out_ref, phys_sc,
):
    variables, levels, rows, cols = x_ref.shape
    pairs = variables * levels
    whole = rows * cols
    na, nb = a_ref.shape[1], b_ref.shape[1]
    helping = jnp.max(got_ref[pairs:, :].astype(f32)) > 0.5

    @pl.when(helping)
    def _():
        phys_sc[:, :nb] = b_ref[...]
        phys_sc[:, nb:] = jnp.zeros((pairs, whole - nb), phys_sc.dtype)

    @pl.when(jnp.logical_not(helping))
    def _():
        phys_sc[:, :na] = a_ref[...]
        phys_sc[:, na : na + nb] = b_ref[...]
        phys_sc[:, na + nb :] = back_ref[...]

    level = iota((levels, levels), 0) == iota((levels, levels), 1)
    rate = jnp.concatenate(
        [
            jnp.sum(
                jnp.where(level, jnp.broadcast_to(diffusion_ref[f : f + 1, :], (levels, levels)), 0.0),
                axis=1,
                keepdims=True,
            )
            for f in range(variables)
        ],
        axis=0,
    )
    state = [x_ref[:, :, y, :].reshape(pairs, cols) for y in range(rows)]
    band = place_ref[0]
    even = place_ref[1] % 2 == 0
    shift = na % LANES
    inner = got_ref[:pairs, na - shift :].astype(f32)
    outer = swap_ref[...].astype(f32)
    above = jnp.where(band > 0, north_ref[...].astype(f32), 0.0)
    below = jnp.where(band < bands - 1, south_ref[...].astype(f32), 0.0)
    lane = iota((pairs, cols), 1)
    for y in range(rows):
        here = state[y]
        near, far = inner[:, shift + y : shift + y + 1], outer[:, y : y + 1]
        west, east = jnp.where(even, far, near), jnp.where(even, near, far)
        left = jnp.where(lane == 0, west, pltpu.roll(here, 1, 1))
        right = jnp.where(lane == cols - 1, east, pltpu.roll(here, cols - 1, 1))
        up = state[y - 1] if y > 0 else above
        down = state[y + 1] if y < rows - 1 else below
        laplace = left + right + up + down - 4.0 * here
        span = slice(y * cols, (y + 1) * cols)
        live = work_ref[pairs : pairs + 1, span].astype(f32) > 0.5
        tend = jnp.where(live, phys_sc[:, span].astype(f32), 0.0)
        out_ref[:, :, y, :] = (here + rate * laplace + tend).reshape(variables, levels, cols)


VMEM = pl.BlockSpec(memory_space=pltpu.VMEM)
SMEM = pl.BlockSpec(memory_space=pltpu.SMEM)


def shape(dims, dtype=bf16):
    return jax.ShapeDtypeStruct(dims, dtype)


def network(phase, cols, given, work, got, weights, dims):
    variables, levels = dims
    table, heads, norm_gains, w_qkv, w_out, w_up, w_down, head_t = weights
    pairs = variables * levels
    depth = table.shape[0]
    return pl.pallas_call(
        functools.partial(network_kernel, phase, dims, given),
        out_shape=shape((pairs, cols)),
        in_specs=[VMEM] * 10,
        out_specs=VMEM,
        scratch_shapes=[
            pltpu.VMEM((depth, cols), bf16),
            pltpu.VMEM((work.shape[0] - pairs, cols), f32),
        ],
        compiler_params=pltpu.CompilerParams(vmem_limit_bytes=16 << 20),
        cost_estimate=pl.CostEstimate(
            flops=3_000_000_000, bytes_accessed=2_000_000, transcendentals=4_000_000
        ),
        name="column_physics",
    )(work, got, table, heads, norm_gains, w_qkv, w_out, w_up, w_down, head_t)


def load_kernel(after_ref, embed_ref, level_ref, *refs):
    count = (len(refs) - 3) // 2
    sems = refs[-1]
    table_ref, heads_ref = refs[2 * count : 2 * count + 2]
    copies = [
        pltpu.make_async_copy(refs[i], refs[count + i], sems.at[i]) for i in range(count)
    ]
    for copy in copies:
        copy.start()
    variables, levels = embed_ref.shape[0], level_ref.shape[0]
    depth, width = table_ref.shape
    pairs = variables * levels
    head_size = width // HEADS
    for f in range(variables):
        table_ref[f * levels : (f + 1) * levels, :] = jnp.broadcast_to(
            embed_ref[f : f + 1, :].astype(f32), (levels, width)
        ).astype(bf16)
    table_ref[pairs : pairs + levels, :] = level_ref[...]
    table_ref[pairs + levels :, :] = jnp.zeros((depth - pairs - levels, width), bf16)
    same = iota((width, width), 0) // head_size == iota((width, width), 1) // head_size
    heads_ref[...] = jnp.where(same, 1.0 / head_size, 0.0).astype(bf16)
    for copy in copies:
        copy.wait()


def load(after, w_embed, level_embed, *arrays):
    hbm = pl.BlockSpec(memory_space=pltpu.HBM)
    variables, width = w_embed.shape
    levels = level_embed.shape[0]
    depth = -(-(variables + 1) * levels // 64) * 64
    outs = [shape(w.shape, w.dtype) for w in arrays]
    outs += [shape((depth, width)), shape((width, width))]
    *loaded, table, heads = pl.pallas_call(
        load_kernel,
        out_shape=outs,
        in_specs=[VMEM] * 3 + [hbm] * len(arrays),
        out_specs=[VMEM] * len(outs),
        scratch_shapes=[pltpu.SemaphoreType.DMA((len(arrays),))],
        compiler_params=pltpu.CompilerParams(vmem_limit_bytes=8 << 20),
        cost_estimate=pl.CostEstimate(flops=0, bytes_accessed=4_000_000, transcendentals=0),
        name="load_weights",
    )(
        after,
        w_embed,
        level_embed,
        *(pltpu.with_memory_space_constraint(w, pltpu.HBM) for w in arrays),
    )
    return table, heads, *loaded


def pack(place, block_counts, conv_flags, column_state, given, two_bands):
    variables, levels, rows, cols = column_state.shape
    pairs = variables * levels
    tall = pairs + 8
    row = shape((pairs, cols))
    edge = shape((pairs, LANES))
    wide = given - given % LANES + LANES
    outs = [shape((tall, rows * cols)), shape((tall, wide))]
    outs += [row] if two_bands else [row, row]
    outs += [edge]

    def kernel(*refs):
        if two_bands:
            refs = refs[:6] + (None,) + refs[6:]
        pack_kernel(given, *refs)

    return pl.pallas_call(
        kernel,
        out_shape=outs,
        in_specs=[SMEM, SMEM, VMEM, VMEM],
        out_specs=[VMEM] * len(outs),
        compiler_params=pltpu.CompilerParams(vmem_limit_bytes=8 << 20),
        name="pack",
    )(place, block_counts, conv_flags, column_state)


def shards(column_state, conv_flags, block_counts, diffusion, *weights):
    variables, levels, rows, cols = column_state.shape
    pairs = variables * levels
    weights = weights[:-1] + (weights[-1].T,)
    tiles, bands = lax.axis_size("tile"), lax.axis_size("band")
    given = cols + 3 * cols // 8
    kept = rows * cols - 2 * given
    assert tiles % 2 == 0 and given % LANES + rows <= LANES
    place = jnp.stack([lax.axis_index("band"), lax.axis_index("tile")]).astype(jnp.int32)
    packed = pack(place, block_counts, conv_flags, column_state, given, bands == 2)
    work, give = packed[:2]
    pairing = [(i, i ^ 1) for i in range(tiles)]
    across = [(i, (i + 1 if i % 2 else i - 1) % tiles) for i in range(tiles)]
    got = lax.ppermute(give, "tile", pairing)
    swap = lax.ppermute(packed[-1], "tile", across)
    weights = load(packed[-1], *weights)
    a = network(0, given, given, work, got, weights, (variables, levels))
    a, *edges = lax.optimization_barrier((a, *packed[2:-1]))
    back = lax.ppermute(a, "tile", pairing)
    if bands == 2:
        north = south = lax.ppermute(edges[0], "band", [(0, 1), (1, 0)])
    else:
        south = lax.ppermute(edges[0], "band", [(i + 1, i) for i in range(bands - 1)])
        north = lax.ppermute(edges[1], "band", [(i, i + 1) for i in range(bands - 1)])
    b = network(1, kept, given, work, got, weights, (variables, levels))

    def kernel(place_ref, *refs):
        final_kernel(place_ref, bands, *refs)

    return pl.pallas_call(
        kernel,
        out_shape=shape(column_state.shape, f32),
        in_specs=[SMEM] + [VMEM] * 10,
        out_specs=VMEM,
        scratch_shapes=[pltpu.VMEM((pairs, rows * cols), bf16)],
        compiler_params=pltpu.CompilerParams(vmem_limit_bytes=8 << 20),
        name="combine",
    )(place, column_state, diffusion, work, got, a, b, back, south, north, swap)


def solution(mesh):
    placed = (
        P(None, None, "band", "tile"),
        P("band", "tile"),
        P("band", "tile"),
        P(),
        P(),
        P(),
        P(),
        P(),
        P(),
        P(),
        P(),
        P(),
    )
    return jax.shard_map(
        shards, mesh=mesh, in_specs=placed, out_specs=P(None, None, "band", "tile"), check_vma=False
    )
```

```python
import functools

import jax
import jax.numpy as jnp
from jax import lax
from jax.experimental import pallas as pl
from jax.experimental.pallas import tpu as pltpu
from jax.sharding import PartitionSpec as P

HEADS = 4
CHAIN = 32
CHAINS = 6
GROUP = 8
LANES = 128
bf16 = jnp.bfloat16
f32 = jnp.float32


def dot(a, b):
    return jnp.dot(a, b, preferred_element_type=f32)


def dot_nt(a, b):
    return lax.dot_general(a, b, (((1,), (1,)), ((), ())), preferred_element_type=f32)


def iota(shape, dim):
    return lax.broadcasted_iota(jnp.int32, shape, dim)


def rms(values, gain):
    mean = jnp.mean(values * values, axis=-1, keepdims=True)
    return values * lax.rsqrt(mean + 1e-05) * gain


def pack_kernel(
    given, place_ref, count_ref, flags_ref, x_ref, work_ref, give_ref, south_ref, north_ref, swap_ref
):
    variables, levels, rows, cols = x_ref.shape
    pairs = variables * levels
    live = (flags_ref[...] == 1) & (iota((rows, cols), 0) < count_ref[0, 0])
    live = jnp.where(live, 1.0, 0.0)
    extra = work_ref.shape[0] - pairs
    west, east = [], []
    for y in range(rows):
        here = slice(y * cols, (y + 1) * cols)
        state = x_ref[:, :, y, :].reshape(pairs, cols)
        work_ref[:pairs, here] = state.astype(bf16)
        work_ref[pairs:, here] = jnp.where(
            iota((extra, cols), 0) == 0, live[y : y + 1, :], 0.0
        ).astype(bf16)
        west.append(state[:, :LANES])
        east.append(state[:, cols - LANES :])
    first, last = work_ref[:pairs, :cols], work_ref[:pairs, (rows - 1) * cols :]
    if south_ref is None:
        north_ref[...] = jnp.where(place_ref[0] == 0, last, first)
    else:
        north_ref[...] = last
        south_ref[...] = first
    odd = (place_ref[1] % 2).astype(f32)
    even = 1.0 - odd
    lane = iota((pairs, LANES), 1)
    shift = given % LANES
    lows = jnp.zeros((pairs, LANES), f32)
    highs = jnp.zeros((pairs, LANES), f32)
    for y in range(rows):
        lows = jnp.where(lane == y, pltpu.roll(west[y], y, 1) if y else west[y], lows)
        highs = jnp.where(lane == y, pltpu.roll(east[y], y + 1, 1), highs)
    swap_ref[...] = (lows * even + highs * odd).astype(bf16)
    inner = pltpu.roll(lows * odd + highs * even, shift, 1)
    whole = rows * cols
    give_ref[:, :given] = work_ref[:, whole - given :]
    tail = given - shift
    mixed = jnp.where(lane < shift, give_ref[:pairs, tail:].astype(f32), inner)
    give_ref[:pairs, tail:] = mixed.astype(bf16)
    extra_lane = iota((extra, LANES), 1)
    mask = jnp.where(extra_lane < shift, give_ref[pairs:, tail:].astype(f32), 0.0)
    give_ref[pairs:, tail:] = mask.astype(bf16)


def network_kernel(
    phase,
    dims,
    given,
    work_ref,
    got_ref,
    table_sc,
    heads_sc,
    gains_ref,
    qkv_ref,
    out_w_ref,
    up_ref,
    down_ref,
    head_ref,
    phys_ref,
    inputs_sc,
    pos_sc,
):
    variables, levels = dims
    width = out_w_ref.shape[0]
    cols = phys_ref.shape[1]
    head_size = width // HEADS
    pairs = variables * levels
    depth = inputs_sc.shape[0]
    tokens = levels * CHAIN
    group_tokens = levels * GROUP
    zero = jnp.zeros((), bf16)

    before = jnp.where(iota((cols, cols), 0) < iota((cols, cols), 1), 1.0, 0.0).astype(bf16)
    inputs_sc[pairs:, :] = jnp.where(
        iota((depth - pairs, cols), 0) < levels, 1.0, 0.0
    ).astype(bf16)

    def sum_of(source, start):
        return jnp.sum(source[pairs:, start : start + cols].astype(f32)).astype(jnp.int32)

    helped = jnp.sum(got_ref[pairs:, :].astype(f32)).astype(jnp.int32)
    helping = helped > 0
    if phase == 0:
        choices = ((got_ref, 0), (work_ref, 0))
        total_live = jnp.where(helping, helped, sum_of(work_ref, 0))
    else:
        choices = ((work_ref, 0), (work_ref, given))
        total_live = jnp.where(helping, sum_of(work_ref, 0), sum_of(work_ref, given))

    def take(source, start):
        inputs_sc[:pairs, :] = source[:pairs, start : start + cols]
        pos_sc[...] = source[pairs:, start : start + cols].astype(f32)

    pl.when(helping)(functools.partial(take, *choices[0]))
    pl.when(jnp.logical_not(helping))(functools.partial(take, *choices[1]))
    live = pos_sc[...]
    place = dot(live.astype(bf16), before)
    pos_sc[...] = jnp.where(live > 0.5, place, -1.0)
    phys_ref[...] = jnp.zeros(phys_ref.shape, phys_ref.dtype)
    def embed(packed):
        lane_level = iota((levels, depth), 1) % levels
        parts = []
        for g in range(CHAIN // GROUP):
            rows_g = packed[g * GROUP : (g + 1) * GROUP, :]
            for l in range(levels):
                parts.append(jnp.where(lane_level == l, rows_g, 0.0))
        return dot(jnp.concatenate(parts, axis=0).astype(bf16), table_sc[...])

    def project(hidden):
        normed = rms(hidden, gains_ref[0:1, :]).astype(bf16)
        queries = dot(normed, qkv_ref[:, :width])
        keys = dot(normed, qkv_ref[:, width : 2 * width])
        values = dot(normed, qkv_ref[:, 2 * width :]).astype(bf16)
        return queries, keys, values

    def normalize(queries, keys):
        both = jnp.concatenate([queries, keys], axis=0)
        mean = dot((both * both).astype(bf16), heads_sc[...])
        q_mean, k_mean = mean[:tokens], mean[tokens:]
        queries = (queries * (lax.rsqrt(q_mean + 1e-05) * head_size**-0.5)).astype(bf16)
        keys = (keys * lax.rsqrt(k_mean + 1e-05)).astype(bf16)
        return queries, keys

    def split(part):
        head_of = iota((group_tokens, width), 1) // head_size
        return jnp.concatenate(
            [jnp.where(head_of == h, part, zero) for h in range(HEADS)], axis=0
        )

    def attend(parts):
        same = (iota((group_tokens, width), 0) % GROUP) == (iota((group_tokens, width), 1) % GROUP)
        groups = [
            (c, slice(g * group_tokens, (g + 1) * group_tokens))
            for c in range(len(parts))
            for g in range(CHAIN // GROUP)
        ]
        scores = [dot_nt(parts[c][0][h], split(parts[c][1][h])) for c, h in groups]
        probs = [jnp.where(same, jnp.exp(v), 0.0).astype(bf16) for v in scores]
        mixed = [dot(p, split(parts[c][2][h])) for p, (c, h) in zip(probs, groups)]
        total = dot(jnp.concatenate(probs, axis=0), heads_sc[...]) * head_size
        mixed = (jnp.concatenate(mixed, axis=0) / total).astype(bf16)
        return [mixed[c * tokens : (c + 1) * tokens] for c in range(len(parts))]

    def feed(after_attn):
        normed = (rms(after_attn, gains_ref[1:2, :]) * 0.5).astype(bf16)
        inner = dot(normed, up_ref[...])
        inner = (inner + inner * jnp.tanh(inner)).astype(bf16)
        return after_attn + dot(inner, down_ref[...])

    def finish(after_mlp):
        normed = rms(after_mlp, gains_ref[2:3, :]).astype(bf16)
        tend = dot_nt(head_ref[...], normed)
        level_of = (iota((levels, tokens), 1) // GROUP) % levels == iota((levels, tokens), 0)
        return jnp.concatenate(
            [
                jnp.where(level_of, jnp.broadcast_to(tend[f : f + 1, :], (levels, tokens)), 0.0)
                for f in range(variables)
            ],
            axis=0,
        ).astype(bf16)

    def evaluate(start, chains):
        slots = (iota((chains * CHAIN, cols), 0) + start).astype(f32)
        pick = jnp.where(pos_sc[0:1, :] == slots, 1.0, 0.0)
        packed = dot_nt(pick.astype(bf16), inputs_sc[...])
        span = range(chains)
        hidden = [embed(packed[i * CHAIN : (i + 1) * CHAIN, :]) for i in span]
        qkv = [project(h) for h in hidden]
        qk = [normalize(q, k) for q, k, _ in qkv]
        mixed = attend([(*qk[i], qkv[i][2]) for i in span])
        after = [hidden[i] + dot(mixed[i], out_w_ref[...]) for i in span]
        after = [feed(a) for a in after]
        placed = jnp.concatenate([finish(a) for a in after], axis=1)
        parts = []
        for g in range(chains * CHAIN // GROUP):
            part = pick[g * GROUP : (g + 1) * GROUP, :]
            part = jnp.concatenate([part, part], axis=0).astype(bf16)
            parts.extend([part] * (levels // 2))
        phys_ref[...] += dot(placed, jnp.concatenate(parts, axis=0)).astype(phys_ref.dtype)

    units = (total_live + (CHAIN - 1)) // CHAIN
    rounds = (units + 1) // CHAINS

    def body(t, carry):
        evaluate(t * (CHAIN * CHAINS), CHAINS)
        return carry

    lax.fori_loop(0, rounds, body, 0)
    rest = units - rounds * CHAINS
    for chains in range(2, CHAINS - 1, 2):
        pl.when((rest == chains) | (rest == chains - 1))(
            functools.partial(evaluate, rounds * (CHAIN * CHAINS), chains)
        )


def final_kernel(
    place_ref, bands, x_ref, diffusion_ref, work_ref, got_ref, a_ref, b_ref, back_ref,
    south_ref, north_ref, swap_ref, out_ref, phys_sc, result_sc, sems,
):
    variables, levels, rows, cols = x_ref.shape
    pairs = variables * levels
    whole = rows * cols
    na, nb = a_ref.shape[1], b_ref.shape[1]
    helping = jnp.max(got_ref[pairs:, :].astype(f32)) > 0.5

    @pl.when(helping)
    def _():
        phys_sc[:, :nb] = b_ref[...]
        phys_sc[:, nb:] = jnp.zeros((pairs, whole - nb), phys_sc.dtype)

    @pl.when(jnp.logical_not(helping))
    def _():
        phys_sc[:, :na] = a_ref[...]
        phys_sc[:, na : na + nb] = b_ref[...]
        phys_sc[:, na + nb :] = back_ref[...]

    level = iota((levels, levels), 0) == iota((levels, levels), 1)
    rate = jnp.concatenate(
        [
            jnp.sum(
                jnp.where(level, jnp.broadcast_to(diffusion_ref[f : f + 1, :], (levels, levels)), 0.0),
                axis=1,
                keepdims=True,
            )
            for f in range(variables)
        ],
        axis=0,
    )
    state = [x_ref[:, :, y, :].reshape(pairs, cols) for y in range(rows)]
    band = place_ref[0]
    odd = (place_ref[1] % 2).astype(f32)
    even = 1.0 - odd
    shift = na % LANES
    near = pltpu.roll(got_ref[:pairs, na - shift :].astype(f32), LANES - shift, 1)
    far = swap_ref[...].astype(f32)
    west, east = far * even + near * odd, near * even + far * odd
    above = jnp.where(band > 0, north_ref[...].astype(f32), 0.0)
    below = jnp.where(band < bands - 1, south_ref[...].astype(f32), 0.0)
    lane = iota((levels, cols), 1)
    copies = []
    for f in range(variables):
        part = slice(f * levels, (f + 1) * levels)
        state = [x_ref[f, :, y, :] for y in range(rows)]
        for y in range(rows):
            here = state[y]
            left = jnp.where(lane == 0, west[part, y : y + 1], pltpu.roll(here, 1, 1))
            right = jnp.where(
                lane == cols - 1, east[part, y : y + 1], pltpu.roll(here, cols - 1, 1)
            )
            up = state[y - 1] if y > 0 else above[part]
            down = state[y + 1] if y < rows - 1 else below[part]
            laplace = left + right + up + down - 4.0 * here
            span = slice(y * cols, (y + 1) * cols)
            live = work_ref[pairs : pairs + 1, span].astype(f32) > 0.5
            tend = jnp.where(live, phys_sc[part, span].astype(f32), 0.0)
            result_sc[f, :, y, :] = here + rate[part] * laplace + tend
        copies.append(pltpu.make_async_copy(result_sc.at[f], out_ref.at[f], sems.at[f]))
        if f > 0:
            copies[f - 1].start()
    copies[-1].start()
    for copy in copies:
        copy.wait()


VMEM = pl.BlockSpec(memory_space=pltpu.VMEM)
SMEM = pl.BlockSpec(memory_space=pltpu.SMEM)


def shape(dims, dtype=bf16):
    return jax.ShapeDtypeStruct(dims, dtype)


def network(phase, cols, given, work, got, weights, dims):
    variables, levels = dims
    table, heads, norm_gains, w_qkv, w_out, w_up, w_down, head_t = weights
    pairs = variables * levels
    depth = table.shape[0]
    return pl.pallas_call(
        functools.partial(network_kernel, phase, dims, given),
        out_shape=shape((pairs, cols)),
        in_specs=[VMEM] * 10,
        out_specs=VMEM,
        scratch_shapes=[
            pltpu.VMEM((depth, cols), bf16),
            pltpu.VMEM((work.shape[0] - pairs, cols), f32),
        ],
        compiler_params=pltpu.CompilerParams(vmem_limit_bytes=16 << 20),
        cost_estimate=pl.CostEstimate(
            flops=3_000_000_000, bytes_accessed=2_000_000, transcendentals=4_000_000
        ),
        name="column_physics",
    )(work, got, table, heads, norm_gains, w_qkv, w_out, w_up, w_down, head_t)


def load_kernel(after_ref, embed_ref, level_ref, *refs):
    count = (len(refs) - 3) // 2
    sems = refs[-1]
    table_ref, heads_ref = refs[2 * count : 2 * count + 2]
    copies = [
        pltpu.make_async_copy(refs[i], refs[count + i], sems.at[i]) for i in range(count)
    ]
    for copy in copies:
        copy.start()
    variables, levels = embed_ref.shape[0], level_ref.shape[0]
    depth, width = table_ref.shape
    pairs = variables * levels
    head_size = width // HEADS
    for f in range(variables):
        table_ref[f * levels : (f + 1) * levels, :] = jnp.broadcast_to(
            embed_ref[f : f + 1, :].astype(f32), (levels, width)
        ).astype(bf16)
    table_ref[pairs : pairs + levels, :] = level_ref[...]
    table_ref[pairs + levels :, :] = jnp.zeros((depth - pairs - levels, width), bf16)
    same = iota((width, width), 0) // head_size == iota((width, width), 1) // head_size
    heads_ref[...] = jnp.where(same, 1.0 / head_size, 0.0).astype(bf16)
    for copy in copies:
        copy.wait()


def load(after, w_embed, level_embed, *arrays):
    hbm = pl.BlockSpec(memory_space=pltpu.HBM)
    variables, width = w_embed.shape
    levels = level_embed.shape[0]
    depth = -(-(variables + 1) * levels // 64) * 64
    outs = [shape(w.shape, w.dtype) for w in arrays]
    outs += [shape((depth, width)), shape((width, width))]
    *loaded, table, heads = pl.pallas_call(
        load_kernel,
        out_shape=outs,
        in_specs=[VMEM] * 3 + [hbm] * len(arrays),
        out_specs=[VMEM] * len(outs),
        scratch_shapes=[pltpu.SemaphoreType.DMA((len(arrays),))],
        compiler_params=pltpu.CompilerParams(vmem_limit_bytes=8 << 20),
        cost_estimate=pl.CostEstimate(flops=0, bytes_accessed=4_000_000, transcendentals=0),
        name="load_weights",
    )(
        after,
        w_embed,
        level_embed,
        *(pltpu.with_memory_space_constraint(w, pltpu.HBM) for w in arrays),
    )
    return table, heads, *loaded


def pack(place, block_counts, conv_flags, column_state, given, two_bands):
    variables, levels, rows, cols = column_state.shape
    pairs = variables * levels
    tall = pairs + 8
    row = shape((pairs, cols))
    edge = shape((pairs, LANES))
    wide = given - given % LANES + LANES
    outs = [shape((tall, rows * cols)), shape((tall, wide))]
    outs += [row] if two_bands else [row, row]
    outs += [edge]

    def kernel(*refs):
        if two_bands:
            refs = refs[:6] + (None,) + refs[6:]
        pack_kernel(given, *refs)

    return pl.pallas_call(
        kernel,
        out_shape=outs,
        in_specs=[SMEM, SMEM, VMEM, VMEM],
        out_specs=[VMEM] * len(outs),
        compiler_params=pltpu.CompilerParams(vmem_limit_bytes=8 << 20),
        name="pack",
    )(place, block_counts, conv_flags, column_state)


def shards(column_state, conv_flags, block_counts, diffusion, *weights):
    variables, levels, rows, cols = column_state.shape
    pairs = variables * levels
    weights = weights[:-1] + (weights[-1].T,)
    tiles, bands = lax.axis_size("tile"), lax.axis_size("band")
    given = cols + 3 * cols // 8
    kept = rows * cols - 2 * given
    assert tiles % 2 == 0 and given % LANES + rows <= LANES
    place = jnp.stack([lax.axis_index("band"), lax.axis_index("tile")]).astype(jnp.int32)
    packed = pack(place, block_counts, conv_flags, column_state, given, bands == 2)
    work, give = packed[:2]
    pairing = [(i, i ^ 1) for i in range(tiles)]
    across = [(i, (i + 1 if i % 2 else i - 1) % tiles) for i in range(tiles)]
    got = lax.ppermute(give, "tile", pairing)
    swap = lax.ppermute(packed[-1], "tile", across)
    weights = load(packed[-1], *weights)
    a = network(0, given, given, work, got, weights, (variables, levels))
    a, *edges = lax.optimization_barrier((a, *packed[2:-1]))
    back = lax.ppermute(a, "tile", pairing)
    if bands == 2:
        north = south = lax.ppermute(edges[0], "band", [(0, 1), (1, 0)])
    else:
        south = lax.ppermute(edges[0], "band", [(i + 1, i) for i in range(bands - 1)])
        north = lax.ppermute(edges[1], "band", [(i, i + 1) for i in range(bands - 1)])
    b = network(1, kept, given, work, got, weights, (variables, levels))

    def kernel(place_ref, *refs):
        final_kernel(place_ref, bands, *refs)

    return pl.pallas_call(
        kernel,
        out_shape=shape(column_state.shape, f32),
        in_specs=[SMEM] + [VMEM] * 10,
        out_specs=pl.BlockSpec(memory_space=pltpu.HBM),
        scratch_shapes=[
            pltpu.VMEM((pairs, rows * cols), bf16),
            pltpu.VMEM(column_state.shape, f32),
            pltpu.SemaphoreType.DMA((variables,)),
        ],
        compiler_params=pltpu.CompilerParams(vmem_limit_bytes=8 << 20),
        name="combine",
    )(place, column_state, diffusion, work, got, a, b, back, south, north, swap)


def solution(mesh):
    placed = (
        P(None, None, "band", "tile"),
        P("band", "tile"),
        P("band", "tile"),
        P(),
        P(),
        P(),
        P(),
        P(),
        P(),
        P(),
        P(),
        P(),
    )
    return jax.shard_map(
        shards, mesh=mesh, in_specs=placed, out_specs=P(None, None, "band", "tile"), check_vma=False
    )
```

```python
import functools

import jax
import jax.numpy as jnp
from jax import lax
from jax.experimental import pallas as pl
from jax.experimental.pallas import tpu as pltpu
from jax.sharding import PartitionSpec as P

HEADS = 4
CHAIN = 32
CHAINS = 6
GROUP = 8
LANES = 128
bf16 = jnp.bfloat16
f32 = jnp.float32


def dot(a, b):
    return jnp.dot(a, b, preferred_element_type=f32)


def dot_nt(a, b):
    return lax.dot_general(a, b, (((1,), (1,)), ((), ())), preferred_element_type=f32)


def iota(shape, dim):
    return lax.broadcasted_iota(jnp.int32, shape, dim)


def rms(values, gain):
    mean = jnp.mean(values * values, axis=-1, keepdims=True)
    return values * lax.rsqrt(mean + 1e-05) * gain


def front_kernel(given, two_bands, count, *refs):
    place_ref, count_ref = refs[:2]
    sources = refs[2 : 6 + count]
    refs = refs[6 + count :]
    work_ref, give_ref = refs[:2]
    south_ref, north_ref = (None, refs[2]) if two_bands else refs[2:4]
    refs = refs[3 if two_bands else 4 :]
    swap_ref, table_ref, heads_ref = refs[:3]
    loaded = refs[3 : 3 + count]
    x_ref, flags_ref, embed_ref, level_ref, sems = refs[3 + count :]
    targets = (x_ref, flags_ref, embed_ref, level_ref, *loaded)
    copies = [
        pltpu.make_async_copy(source, target, sems.at[i])
        for i, (source, target) in enumerate(zip(sources, targets))
    ]
    for copy in copies:
        copy.start()
    copies[1].wait()
    copies[0].wait()
    pack_rows(
        given, place_ref, count_ref, flags_ref, x_ref, work_ref, give_ref, south_ref, north_ref,
        swap_ref,
    )
    copies[2].wait()
    copies[3].wait()
    build_tables(embed_ref, level_ref, table_ref, heads_ref)
    for copy in copies[4:]:
        copy.wait()


def build_tables(embed_ref, level_ref, table_ref, heads_ref):
    variables, levels = embed_ref.shape[0], level_ref.shape[0]
    depth, width = table_ref.shape
    pairs = variables * levels
    head_size = width // HEADS
    for f in range(variables):
        table_ref[f * levels : (f + 1) * levels, :] = jnp.broadcast_to(
            embed_ref[f : f + 1, :].astype(f32), (levels, width)
        ).astype(bf16)
    table_ref[pairs : pairs + levels, :] = level_ref[...]
    table_ref[pairs + levels :, :] = jnp.zeros((depth - pairs - levels, width), bf16)
    same = iota((width, width), 0) // head_size == iota((width, width), 1) // head_size
    heads_ref[...] = jnp.where(same, 1.0 / head_size, 0.0).astype(bf16)


def pack_rows(
    given, place_ref, count_ref, flags_ref, x_ref, work_ref, give_ref, south_ref, north_ref, swap_ref
):
    variables, levels, rows, cols = x_ref.shape
    pairs = variables * levels
    live = (flags_ref[...] == 1) & (iota((rows, cols), 0) < count_ref[0, 0])
    live = jnp.where(live, 1.0, 0.0)
    extra = work_ref.shape[0] - pairs
    west, east = [], []
    for y in range(rows):
        here = slice(y * cols, (y + 1) * cols)
        state = x_ref[:, :, y, :].reshape(pairs, cols)
        work_ref[:pairs, here] = state.astype(bf16)
        work_ref[pairs:, here] = jnp.where(
            iota((extra, cols), 0) == 0, live[y : y + 1, :], 0.0
        ).astype(bf16)
        west.append(state[:, :LANES])
        east.append(state[:, cols - LANES :])
    first, last = work_ref[:pairs, :cols], work_ref[:pairs, (rows - 1) * cols :]
    if south_ref is None:
        north_ref[...] = jnp.where(place_ref[0] == 0, last, first)
    else:
        north_ref[...] = last
        south_ref[...] = first
    odd = (place_ref[1] % 2).astype(f32)
    even = 1.0 - odd
    lane = iota((pairs, LANES), 1)
    shift = given % LANES
    lows = jnp.zeros((pairs, LANES), f32)
    highs = jnp.zeros((pairs, LANES), f32)
    for y in range(rows):
        lows = jnp.where(lane == y, pltpu.roll(west[y], y, 1) if y else west[y], lows)
        highs = jnp.where(lane == y, pltpu.roll(east[y], y + 1, 1), highs)
    swap_ref[...] = (lows * even + highs * odd).astype(bf16)
    inner = pltpu.roll(lows * odd + highs * even, shift, 1)
    whole = rows * cols
    give_ref[:, :given] = work_ref[:, whole - given :]
    tail = given - shift
    mixed = jnp.where(lane < shift, give_ref[:pairs, tail:].astype(f32), inner)
    give_ref[:pairs, tail:] = mixed.astype(bf16)
    extra_lane = iota((extra, LANES), 1)
    mask = jnp.where(extra_lane < shift, give_ref[pairs:, tail:].astype(f32), 0.0)
    give_ref[pairs:, tail:] = mask.astype(bf16)


def network_kernel(
    phase,
    dims,
    given,
    work_ref,
    got_ref,
    table_sc,
    heads_sc,
    gains_ref,
    qkv_ref,
    out_w_ref,
    up_ref,
    down_ref,
    head_ref,
    phys_ref,
    inputs_sc,
    pos_sc,
):
    variables, levels = dims
    width = out_w_ref.shape[0]
    cols = phys_ref.shape[1]
    head_size = width // HEADS
    pairs = variables * levels
    depth = inputs_sc.shape[0]
    tokens = levels * CHAIN
    group_tokens = levels * GROUP
    zero = jnp.zeros((), bf16)

    before = jnp.where(iota((cols, cols), 0) < iota((cols, cols), 1), 1.0, 0.0).astype(bf16)
    inputs_sc[pairs:, :] = jnp.where(
        iota((depth - pairs, cols), 0) < levels, 1.0, 0.0
    ).astype(bf16)

    def sum_of(source, start):
        return jnp.sum(source[pairs:, start : start + cols].astype(f32)).astype(jnp.int32)

    helped = jnp.sum(got_ref[pairs:, :].astype(f32)).astype(jnp.int32)
    helping = helped > 0
    if phase == 0:
        choices = ((got_ref, 0), (work_ref, 0))
        total_live = jnp.where(helping, helped, sum_of(work_ref, 0))
    else:
        choices = ((work_ref, 0), (work_ref, given))
        total_live = jnp.where(helping, sum_of(work_ref, 0), sum_of(work_ref, given))

    def take(source, start):
        inputs_sc[:pairs, :] = source[:pairs, start : start + cols]
        pos_sc[...] = source[pairs:, start : start + cols].astype(f32)

    pl.when(helping)(functools.partial(take, *choices[0]))
    pl.when(jnp.logical_not(helping))(functools.partial(take, *choices[1]))
    live = pos_sc[...]
    place = dot(live.astype(bf16), before)
    pos_sc[...] = jnp.where(live > 0.5, place, -1.0)
    phys_ref[...] = jnp.zeros(phys_ref.shape, phys_ref.dtype)
    def embed(packed):
        lane_level = iota((levels, depth), 1) % levels
        parts = []
        for g in range(CHAIN // GROUP):
            rows_g = packed[g * GROUP : (g + 1) * GROUP, :]
            for l in range(levels):
                parts.append(jnp.where(lane_level == l, rows_g, 0.0))
        return dot(jnp.concatenate(parts, axis=0).astype(bf16), table_sc[...])

    def project(hidden):
        normed = rms(hidden, gains_ref[0:1, :]).astype(bf16)
        queries = dot(normed, qkv_ref[:, :width])
        keys = dot(normed, qkv_ref[:, width : 2 * width])
        values = dot(normed, qkv_ref[:, 2 * width :]).astype(bf16)
        return queries, keys, values

    def normalize(queries, keys):
        both = jnp.concatenate([queries, keys], axis=0)
        mean = dot((both * both).astype(bf16), heads_sc[...])
        q_mean, k_mean = mean[:tokens], mean[tokens:]
        queries = (queries * (lax.rsqrt(q_mean + 1e-05) * head_size**-0.5)).astype(bf16)
        keys = (keys * lax.rsqrt(k_mean + 1e-05)).astype(bf16)
        return queries, keys

    def split(part):
        head_of = iota((group_tokens, width), 1) // head_size
        return jnp.concatenate(
            [jnp.where(head_of == h, part, zero) for h in range(HEADS)], axis=0
        )

    def attend(parts):
        same = (iota((group_tokens, width), 0) % GROUP) == (iota((group_tokens, width), 1) % GROUP)
        groups = [
            (c, slice(g * group_tokens, (g + 1) * group_tokens))
            for c in range(len(parts))
            for g in range(CHAIN // GROUP)
        ]
        scores = [dot_nt(parts[c][0][h], split(parts[c][1][h])) for c, h in groups]
        probs = [jnp.where(same, jnp.exp(v), 0.0).astype(bf16) for v in scores]
        mixed = [dot(p, split(parts[c][2][h])) for p, (c, h) in zip(probs, groups)]
        total = dot(jnp.concatenate(probs, axis=0), heads_sc[...]) * head_size
        mixed = (jnp.concatenate(mixed, axis=0) / total).astype(bf16)
        return [mixed[c * tokens : (c + 1) * tokens] for c in range(len(parts))]

    def feed(after_attn):
        normed = (rms(after_attn, gains_ref[1:2, :]) * 0.5).astype(bf16)
        inner = dot(normed, up_ref[...])
        inner = (inner + inner * jnp.tanh(inner)).astype(bf16)
        return after_attn + dot(inner, down_ref[...])

    def finish(after_mlp):
        normed = rms(after_mlp, gains_ref[2:3, :]).astype(bf16)
        tend = dot_nt(head_ref[...], normed)
        level_of = (iota((levels, tokens), 1) // GROUP) % levels == iota((levels, tokens), 0)
        return jnp.concatenate(
            [
                jnp.where(level_of, jnp.broadcast_to(tend[f : f + 1, :], (levels, tokens)), 0.0)
                for f in range(variables)
            ],
            axis=0,
        ).astype(bf16)

    def evaluate(start, chains):
        slots = (iota((chains * CHAIN, cols), 0) + start).astype(f32)
        pick = jnp.where(pos_sc[0:1, :] == slots, 1.0, 0.0)
        packed = dot_nt(pick.astype(bf16), inputs_sc[...])
        span = range(chains)
        hidden = [embed(packed[i * CHAIN : (i + 1) * CHAIN, :]) for i in span]
        qkv = [project(h) for h in hidden]
        qk = [normalize(q, k) for q, k, _ in qkv]
        mixed = attend([(*qk[i], qkv[i][2]) for i in span])
        after = [hidden[i] + dot(mixed[i], out_w_ref[...]) for i in span]
        after = [feed(a) for a in after]
        placed = jnp.concatenate([finish(a) for a in after], axis=1)
        parts = []
        for g in range(chains * CHAIN // GROUP):
            part = pick[g * GROUP : (g + 1) * GROUP, :]
            part = jnp.concatenate([part, part], axis=0).astype(bf16)
            parts.extend([part] * (levels // 2))
        phys_ref[...] += dot(placed, jnp.concatenate(parts, axis=0)).astype(phys_ref.dtype)

    units = (total_live + (CHAIN - 1)) // CHAIN
    rounds = (units + 1) // CHAINS

    def body(t, carry):
        evaluate(t * (CHAIN * CHAINS), CHAINS)
        return carry

    lax.fori_loop(0, rounds, body, 0)
    rest = units - rounds * CHAINS
    for chains in range(2, CHAINS - 1, 2):
        pl.when((rest == chains) | (rest == chains - 1))(
            functools.partial(evaluate, rounds * (CHAIN * CHAINS), chains)
        )


def final_kernel(
    place_ref, bands, x_ref, diffusion_ref, work_ref, got_ref, a_ref, b_ref, back_ref,
    south_ref, north_ref, swap_ref, out_ref, phys_sc, result_sc, sems,
):
    variables, levels, rows, cols = x_ref.shape
    pairs = variables * levels
    whole = rows * cols
    na, nb = a_ref.shape[1], b_ref.shape[1]
    helping = jnp.max(got_ref[pairs:, :].astype(f32)) > 0.5

    @pl.when(helping)
    def _():
        phys_sc[:, :nb] = b_ref[...]
        phys_sc[:, nb:] = jnp.zeros((pairs, whole - nb), phys_sc.dtype)

    @pl.when(jnp.logical_not(helping))
    def _():
        phys_sc[:, :na] = a_ref[...]
        phys_sc[:, na : na + nb] = b_ref[...]
        phys_sc[:, na + nb :] = back_ref[...]

    level = iota((levels, levels), 0) == iota((levels, levels), 1)
    rate = jnp.concatenate(
        [
            jnp.sum(
                jnp.where(level, jnp.broadcast_to(diffusion_ref[f : f + 1, :], (levels, levels)), 0.0),
                axis=1,
                keepdims=True,
            )
            for f in range(variables)
        ],
        axis=0,
    )
    state = [x_ref[:, :, y, :].reshape(pairs, cols) for y in range(rows)]
    band = place_ref[0]
    odd = (place_ref[1] % 2).astype(f32)
    even = 1.0 - odd
    shift = na % LANES
    near = pltpu.roll(got_ref[:pairs, na - shift :].astype(f32), LANES - shift, 1)
    far = swap_ref[...].astype(f32)
    west, east = far * even + near * odd, near * even + far * odd
    above = jnp.where(band > 0, north_ref[...].astype(f32), 0.0)
    below = jnp.where(band < bands - 1, south_ref[...].astype(f32), 0.0)
    lane = iota((levels, cols), 1)
    early = variables // 2
    copies = [
        pltpu.make_async_copy(result_sc.at[here], out_ref.at[here], sems.at[i])
        for i, here in enumerate((pl.ds(0, early), pl.ds(early, variables - early)))
    ]
    for f in range(variables):
        part = slice(f * levels, (f + 1) * levels)
        state = [x_ref[f, :, y, :] for y in range(rows)]
        for y in range(rows):
            here = state[y]
            left = jnp.where(lane == 0, west[part, y : y + 1], pltpu.roll(here, 1, 1))
            right = jnp.where(
                lane == cols - 1, east[part, y : y + 1], pltpu.roll(here, cols - 1, 1)
            )
            up = state[y - 1] if y > 0 else above[part]
            down = state[y + 1] if y < rows - 1 else below[part]
            laplace = left + right + up + down - 4.0 * here
            span = slice(y * cols, (y + 1) * cols)
            live = work_ref[pairs : pairs + 1, span].astype(f32) > 0.5
            tend = jnp.where(live, phys_sc[part, span].astype(f32), 0.0)
            result_sc[f, :, y, :] = here + rate[part] * laplace + tend
        if f == variables - 2:
            copies[0].start()
    copies[1].start()
    for copy in copies:
        copy.wait()


VMEM = pl.BlockSpec(memory_space=pltpu.VMEM)
SMEM = pl.BlockSpec(memory_space=pltpu.SMEM)


def shape(dims, dtype=bf16):
    return jax.ShapeDtypeStruct(dims, dtype)


def network(phase, cols, given, work, got, weights, dims):
    variables, levels = dims
    table, heads, norm_gains, w_qkv, w_out, w_up, w_down, head_t = weights
    pairs = variables * levels
    depth = table.shape[0]
    return pl.pallas_call(
        functools.partial(network_kernel, phase, dims, given),
        out_shape=shape((pairs, cols)),
        in_specs=[VMEM] * 10,
        out_specs=VMEM,
        scratch_shapes=[
            pltpu.VMEM((depth, cols), bf16),
            pltpu.VMEM((work.shape[0] - pairs, cols), f32),
        ],
        compiler_params=pltpu.CompilerParams(vmem_limit_bytes=16 << 20),
        cost_estimate=pl.CostEstimate(
            flops=3_000_000_000, bytes_accessed=2_000_000, transcendentals=4_000_000
        ),
        name="column_physics",
    )(work, got, table, heads, norm_gains, w_qkv, w_out, w_up, w_down, head_t)


def front(place, block_counts, conv_flags, column_state, given, two_bands, weights):
    variables, levels, rows, cols = column_state.shape
    w_embed, level_embed, *arrays = weights
    width = w_embed.shape[1]
    pairs = variables * levels
    depth = -(-(variables + 1) * levels // 64) * 64
    tall = pairs + 8
    wide = given - given % LANES + LANES
    row = shape((pairs, cols))
    outs = [shape((tall, rows * cols)), shape((tall, wide))]
    outs += [row] if two_bands else [row, row]
    outs += [shape((pairs, LANES)), shape((depth, width)), shape((width, width))]
    outs += [shape(w.shape, w.dtype) for w in arrays]
    scratch = [column_state, conv_flags, w_embed, level_embed]
    inputs = scratch + arrays
    hbm = pl.BlockSpec(memory_space=pltpu.HBM)
    return pl.pallas_call(
        functools.partial(front_kernel, given, two_bands, len(arrays)),
        out_shape=outs,
        in_specs=[SMEM, SMEM] + [hbm] * len(inputs),
        out_specs=[VMEM] * len(outs),
        scratch_shapes=[pltpu.VMEM(v.shape, v.dtype) for v in scratch]
        + [pltpu.SemaphoreType.DMA((len(inputs),))],
        compiler_params=pltpu.CompilerParams(vmem_limit_bytes=8 << 20),
        name="pack_and_load",
    )(
        place,
        block_counts,
        *(pltpu.with_memory_space_constraint(v, pltpu.HBM) for v in inputs),
    )


def shards(column_state, conv_flags, block_counts, diffusion, *weights):
    variables, levels, rows, cols = column_state.shape
    pairs = variables * levels
    weights = weights[:-1] + (weights[-1].T,)
    tiles, bands = lax.axis_size("tile"), lax.axis_size("band")
    given = cols + 3 * cols // 8
    kept = rows * cols - 2 * given
    assert tiles % 2 == 0 and given % LANES + rows <= LANES
    place = jnp.stack([lax.axis_index("band"), lax.axis_index("tile")]).astype(jnp.int32)
    packed = front(place, block_counts, conv_flags, column_state, given, bands == 2, weights)
    work, give = packed[:2]
    rows_out, (swap, *weights) = (packed[2:3], packed[3:]) if bands == 2 else (packed[2:4], packed[4:])
    table, heads, gains, *weights = weights
    weights = (table, heads, gains, *weights)
    pairing = [(i, i ^ 1) for i in range(tiles)]
    across = [(i, (i + 1 if i % 2 else i - 1) % tiles) for i in range(tiles)]
    got = lax.ppermute(give, "tile", pairing)
    swap = lax.ppermute(swap, "tile", across)
    a = network(0, given, given, work, got, weights, (variables, levels))
    a, *edges = lax.optimization_barrier((a, *rows_out))
    back = lax.ppermute(a, "tile", pairing)
    if bands == 2:
        north = south = lax.ppermute(edges[0], "band", [(0, 1), (1, 0)])
    else:
        south = lax.ppermute(edges[0], "band", [(i + 1, i) for i in range(bands - 1)])
        north = lax.ppermute(edges[1], "band", [(i, i + 1) for i in range(bands - 1)])
    b = network(1, kept, given, work, got, weights, (variables, levels))

    def kernel(place_ref, *refs):
        final_kernel(place_ref, bands, *refs)

    return pl.pallas_call(
        kernel,
        out_shape=shape(column_state.shape, f32),
        in_specs=[SMEM] + [VMEM] * 10,
        out_specs=pl.BlockSpec(memory_space=pltpu.HBM),
        scratch_shapes=[
            pltpu.VMEM((pairs, rows * cols), bf16),
            pltpu.VMEM(column_state.shape, f32),
            pltpu.SemaphoreType.DMA((2,)),
        ],
        compiler_params=pltpu.CompilerParams(vmem_limit_bytes=8 << 20),
        name="combine",
    )(place, column_state, diffusion, work, got, a, b, back, south, north, swap)


def solution(mesh):
    placed = (
        P(None, None, "band", "tile"),
        P("band", "tile"),
        P("band", "tile"),
        P(),
        P(),
        P(),
        P(),
        P(),
        P(),
        P(),
        P(),
        P(),
    )
    return jax.shard_map(
        shards, mesh=mesh, in_specs=placed, out_specs=P(None, None, "band", "tile"), check_vma=False
    )
```

```python
import functools

import jax
import jax.numpy as jnp
from jax import lax
from jax.experimental import pallas as pl
from jax.experimental.pallas import tpu as pltpu
from jax.sharding import PartitionSpec as P

HEADS = 4
CHAIN = 32
CHAINS = 6
GROUP = 8
LANES = 128
bf16 = jnp.bfloat16
f32 = jnp.float32


def dot(a, b):
    return jnp.dot(a, b, preferred_element_type=f32)


def dot_nt(a, b):
    return lax.dot_general(a, b, (((1,), (1,)), ((), ())), preferred_element_type=f32)


def iota(shape, dim):
    return lax.broadcasted_iota(jnp.int32, shape, dim)


def rms(values, gain):
    mean = jnp.mean(values * values, axis=-1, keepdims=True)
    return values * lax.rsqrt(mean + 1e-05) * gain


def front_kernel(given, two_bands, count, *refs):
    place_ref, count_ref = refs[:2]
    sources = refs[2 : 6 + count]
    refs = refs[6 + count :]
    work_ref, give_ref = refs[:2]
    south_ref, north_ref = (None, refs[2]) if two_bands else refs[2:4]
    refs = refs[3 if two_bands else 4 :]
    swap_ref, table_ref, heads_ref = refs[:3]
    loaded = refs[3 : 3 + count]
    x_ref, flags_ref, embed_ref, level_ref, sems = refs[3 + count :]
    targets = (x_ref, flags_ref, embed_ref, level_ref, *loaded)
    copies = [
        pltpu.make_async_copy(source, target, sems.at[i])
        for i, (source, target) in enumerate(zip(sources, targets))
    ]
    for copy in copies:
        copy.start()
    copies[1].wait()
    copies[0].wait()
    pack_rows(
        given, place_ref, count_ref, flags_ref, x_ref, work_ref, give_ref, south_ref, north_ref,
        swap_ref,
    )
    copies[2].wait()
    copies[3].wait()
    build_tables(embed_ref, level_ref, table_ref, heads_ref)
    for copy in copies[4:]:
        copy.wait()


def build_tables(embed_ref, level_ref, table_ref, heads_ref):
    variables, levels = embed_ref.shape[0], level_ref.shape[0]
    depth, width = table_ref.shape
    pairs = variables * levels
    head_size = width // HEADS
    for f in range(variables):
        table_ref[f * levels : (f + 1) * levels, :] = jnp.broadcast_to(
            embed_ref[f : f + 1, :].astype(f32), (levels, width)
        ).astype(bf16)
    table_ref[pairs : pairs + levels, :] = level_ref[...]
    table_ref[pairs + levels :, :] = jnp.zeros((depth - pairs - levels, width), bf16)
    same = iota((width, width), 0) // head_size == iota((width, width), 1) // head_size
    heads_ref[...] = jnp.where(same, 1.0 / head_size, 0.0).astype(bf16)


def pack_rows(
    given, place_ref, count_ref, flags_ref, x_ref, work_ref, give_ref, south_ref, north_ref, swap_ref
):
    variables, levels, rows, cols = x_ref.shape
    pairs = variables * levels
    live = (flags_ref[...] == 1) & (iota((rows, cols), 0) < count_ref[0, 0])
    live = jnp.where(live, 1.0, 0.0)
    extra = work_ref.shape[0] - pairs
    west, east = [], []
    for y in range(rows):
        here = slice(y * cols, (y + 1) * cols)
        state = x_ref[:, :, y, :].reshape(pairs, cols)
        work_ref[:pairs, here] = state.astype(bf16)
        work_ref[pairs:, here] = jnp.where(
            iota((extra, cols), 0) == 0, live[y : y + 1, :], 0.0
        ).astype(bf16)
        west.append(state[:, :LANES])
        east.append(state[:, cols - LANES :])
    first, last = work_ref[:pairs, :cols], work_ref[:pairs, (rows - 1) * cols :]
    if south_ref is None:
        north_ref[...] = jnp.where(place_ref[0] == 0, last, first)
    else:
        north_ref[...] = last
        south_ref[...] = first
    odd = (place_ref[1] % 2).astype(f32)
    even = 1.0 - odd
    lane = iota((pairs, LANES), 1)
    shift = given % LANES
    lows = jnp.zeros((pairs, LANES), f32)
    highs = jnp.zeros((pairs, LANES), f32)
    for y in range(rows):
        lows = jnp.where(lane == y, pltpu.roll(west[y], y, 1) if y else west[y], lows)
        highs = jnp.where(lane == y, pltpu.roll(east[y], y + 1, 1), highs)
    swap_ref[...] = (lows * even + highs * odd).astype(bf16)
    inner = pltpu.roll(lows * odd + highs * even, shift, 1)
    whole = rows * cols
    give_ref[:, :given] = work_ref[:, whole - given :]
    tail = given - shift
    mixed = jnp.where(lane < shift, give_ref[:pairs, tail:].astype(f32), inner)
    give_ref[:pairs, tail:] = mixed.astype(bf16)
    extra_lane = iota((extra, LANES), 1)
    mask = jnp.where(extra_lane < shift, give_ref[pairs:, tail:].astype(f32), 0.0)
    give_ref[pairs:, tail:] = mask.astype(bf16)


def network_kernel(
    phase,
    dims,
    given,
    work_ref,
    got_ref,
    table_sc,
    heads_sc,
    gains_ref,
    qkv_ref,
    out_w_ref,
    up_ref,
    down_ref,
    head_ref,
    phys_ref,
    inputs_sc,
    pos_sc,
):
    variables, levels = dims
    width = out_w_ref.shape[0]
    cols = phys_ref.shape[1]
    head_size = width // HEADS
    pairs = variables * levels
    depth = inputs_sc.shape[0]
    tokens = levels * CHAIN
    group_tokens = levels * GROUP
    zero = jnp.zeros((), bf16)

    before = jnp.where(iota((cols, cols), 0) < iota((cols, cols), 1), 1.0, 0.0).astype(bf16)
    inputs_sc[pairs:, :] = jnp.where(
        iota((depth - pairs, cols), 0) < levels, 1.0, 0.0
    ).astype(bf16)

    def sum_of(source, start):
        return jnp.sum(source[pairs:, start : start + cols].astype(f32)).astype(jnp.int32)

    helped = jnp.sum(got_ref[pairs:, :].astype(f32)).astype(jnp.int32)
    helping = helped > 0
    if phase == 0:
        choices = ((got_ref, 0), (work_ref, 0))
        total_live = jnp.where(helping, helped, sum_of(work_ref, 0))
    else:
        choices = ((work_ref, 0), (work_ref, given))
        total_live = jnp.where(helping, sum_of(work_ref, 0), sum_of(work_ref, given))

    def take(source, start):
        inputs_sc[:pairs, :] = source[:pairs, start : start + cols]
        pos_sc[...] = source[pairs:, start : start + cols].astype(f32)

    pl.when(helping)(functools.partial(take, *choices[0]))
    pl.when(jnp.logical_not(helping))(functools.partial(take, *choices[1]))
    live = pos_sc[...]
    place = dot(live.astype(bf16), before)
    pos_sc[...] = jnp.where(live > 0.5, place, -1.0)
    phys_ref[...] = jnp.zeros(phys_ref.shape, phys_ref.dtype)
    def embed(packed):
        lane_level = iota((levels, depth), 1) % levels
        parts = []
        for g in range(CHAIN // GROUP):
            rows_g = packed[g * GROUP : (g + 1) * GROUP, :]
            for l in range(levels):
                parts.append(jnp.where(lane_level == l, rows_g, 0.0))
        return dot(jnp.concatenate(parts, axis=0).astype(bf16), table_sc[...])

    def project(hidden):
        normed = rms(hidden, gains_ref[0:1, :]).astype(bf16)
        queries = dot(normed, qkv_ref[:, :width])
        keys = dot(normed, qkv_ref[:, width : 2 * width])
        values = dot(normed, qkv_ref[:, 2 * width :]).astype(bf16)
        return queries, keys, values

    def normalize(queries, keys):
        both = jnp.concatenate([queries, keys], axis=0)
        mean = dot((both * both).astype(bf16), heads_sc[...])
        q_mean, k_mean = mean[:tokens], mean[tokens:]
        queries = (queries * (lax.rsqrt(q_mean + 1e-05) * head_size**-0.5)).astype(bf16)
        keys = (keys * lax.rsqrt(k_mean + 1e-05)).astype(bf16)
        return queries, keys

    def split(part):
        head_of = iota((group_tokens, width), 1) // head_size
        return jnp.concatenate(
            [jnp.where(head_of == h, part, zero) for h in range(HEADS)], axis=0
        )

    def attend(parts):
        same = (iota((group_tokens, width), 0) % GROUP) == (iota((group_tokens, width), 1) % GROUP)
        groups = [
            (c, slice(g * group_tokens, (g + 1) * group_tokens))
            for c in range(len(parts))
            for g in range(CHAIN // GROUP)
        ]
        scores = [dot_nt(parts[c][0][h], split(parts[c][1][h])) for c, h in groups]
        probs = [jnp.where(same, jnp.exp(v), 0.0).astype(bf16) for v in scores]
        mixed = [dot(p, split(parts[c][2][h])) for p, (c, h) in zip(probs, groups)]
        total = dot(jnp.concatenate(probs, axis=0), heads_sc[...]) * head_size
        mixed = (jnp.concatenate(mixed, axis=0) / total).astype(bf16)
        return [mixed[c * tokens : (c + 1) * tokens] for c in range(len(parts))]

    def feed(after_attn):
        normed = (rms(after_attn, gains_ref[1:2, :]) * 0.5).astype(bf16)
        inner = dot(normed, up_ref[...])
        inner = (inner + inner * jnp.tanh(inner)).astype(bf16)
        return after_attn + dot(inner, down_ref[...])

    def finish(after_mlp):
        normed = rms(after_mlp, gains_ref[2:3, :]).astype(bf16)
        tend = dot_nt(head_ref[...], normed)
        level_of = (iota((levels, tokens), 1) // GROUP) % levels == iota((levels, tokens), 0)
        return jnp.concatenate(
            [
                jnp.where(level_of, jnp.broadcast_to(tend[f : f + 1, :], (levels, tokens)), 0.0)
                for f in range(variables)
            ],
            axis=0,
        ).astype(bf16)

    def evaluate(start, chains):
        slots = (iota((chains * CHAIN, cols), 0) + start).astype(f32)
        pick = jnp.where(pos_sc[0:1, :] == slots, 1.0, 0.0)
        packed = dot_nt(pick.astype(bf16), inputs_sc[...])
        span = range(chains)
        hidden = [embed(packed[i * CHAIN : (i + 1) * CHAIN, :]) for i in span]
        qkv = [project(h) for h in hidden]
        qk = [normalize(q, k) for q, k, _ in qkv]
        mixed = attend([(*qk[i], qkv[i][2]) for i in span])
        after = [hidden[i] + dot(mixed[i], out_w_ref[...]) for i in span]
        after = [feed(a) for a in after]
        placed = jnp.concatenate([finish(a) for a in after], axis=1)
        parts = []
        for g in range(chains * CHAIN // GROUP):
            part = pick[g * GROUP : (g + 1) * GROUP, :]
            part = jnp.concatenate([part, part], axis=0).astype(bf16)
            parts.extend([part] * (levels // 2))
        phys_ref[...] += dot(placed, jnp.concatenate(parts, axis=0)).astype(phys_ref.dtype)

    units = (total_live + (CHAIN - 1)) // CHAIN
    rounds = (units + 1) // CHAINS

    def body(t, carry):
        evaluate(t * (CHAIN * CHAINS), CHAINS)
        return carry

    lax.fori_loop(0, rounds, body, 0)
    rest = units - rounds * CHAINS
    for chains in range(2, CHAINS - 1, 2):
        pl.when((rest == chains) | (rest == chains - 1))(
            functools.partial(evaluate, rounds * (CHAIN * CHAINS), chains)
        )


def final_kernel(
    place_ref, bands, x_ref, diffusion_ref, work_ref, got_ref, a_ref, b_ref, back_ref,
    south_ref, north_ref, swap_ref, out_ref, phys_sc, result_sc, sems,
):
    variables, levels, rows, cols = x_ref.shape
    pairs = variables * levels
    whole = rows * cols
    na, nb = a_ref.shape[1], b_ref.shape[1]
    helping = jnp.max(got_ref[pairs:, :].astype(f32)) > 0.5

    @pl.when(helping)
    def _():
        phys_sc[:, :nb] = b_ref[...]
        phys_sc[:, nb:] = jnp.zeros((pairs, whole - nb), phys_sc.dtype)

    @pl.when(jnp.logical_not(helping))
    def _():
        phys_sc[:, :na] = a_ref[...]
        phys_sc[:, na : na + nb] = b_ref[...]
        phys_sc[:, na + nb :] = back_ref[...]

    level = iota((levels, levels), 0) == iota((levels, levels), 1)
    rate = jnp.concatenate(
        [
            jnp.sum(
                jnp.where(level, jnp.broadcast_to(diffusion_ref[f : f + 1, :], (levels, levels)), 0.0),
                axis=1,
                keepdims=True,
            )
            for f in range(variables)
        ],
        axis=0,
    )
    state = [x_ref[:, :, y, :].reshape(pairs, cols) for y in range(rows)]
    band = place_ref[0]
    odd = (place_ref[1] % 2).astype(f32)
    even = 1.0 - odd
    shift = na % LANES
    near = pltpu.roll(got_ref[:pairs, na - shift :].astype(f32), LANES - shift, 1)
    far = swap_ref[...].astype(f32)
    west, east = far * even + near * odd, near * even + far * odd
    above = jnp.where(band > 0, north_ref[...].astype(f32), 0.0)
    below = jnp.where(band < bands - 1, south_ref[...].astype(f32), 0.0)
    lane = iota((levels, cols), 1)
    early = variables // 2
    copies = [
        pltpu.make_async_copy(result_sc.at[here], out_ref.at[here], sems.at[i])
        for i, here in enumerate((pl.ds(0, early), pl.ds(early, variables - early)))
    ]
    for f in range(variables):
        part = slice(f * levels, (f + 1) * levels)
        state = [x_ref[f, :, y, :] for y in range(rows)]
        for y in range(rows):
            here = state[y]
            left = jnp.where(lane == 0, west[part, y : y + 1], pltpu.roll(here, 1, 1))
            right = jnp.where(
                lane == cols - 1, east[part, y : y + 1], pltpu.roll(here, cols - 1, 1)
            )
            up = state[y - 1] if y > 0 else above[part]
            down = state[y + 1] if y < rows - 1 else below[part]
            laplace = left + right + up + down - 4.0 * here
            span = slice(y * cols, (y + 1) * cols)
            live = work_ref[pairs : pairs + 1, span].astype(f32) > 0.5
            tend = jnp.where(live, phys_sc[part, span].astype(f32), 0.0)
            result_sc[f, :, y, :] = here + rate[part] * laplace + tend
        if f == variables - 2:
            copies[0].start()
    copies[1].start()
    for copy in copies:
        copy.wait()


VMEM = pl.BlockSpec(memory_space=pltpu.VMEM)
SMEM = pl.BlockSpec(memory_space=pltpu.SMEM)


def shape(dims, dtype=bf16):
    return jax.ShapeDtypeStruct(dims, dtype)


def network(phase, cols, given, work, got, weights, dims):
    variables, levels = dims
    table, heads, norm_gains, w_qkv, w_out, w_up, w_down, head_t = weights
    pairs = variables * levels
    depth = table.shape[0]
    return pl.pallas_call(
        functools.partial(network_kernel, phase, dims, given),
        out_shape=shape((pairs, cols)),
        in_specs=[VMEM] * 10,
        out_specs=VMEM,
        scratch_shapes=[
            pltpu.VMEM((depth, cols), bf16),
            pltpu.VMEM((work.shape[0] - pairs, cols), f32),
        ],
        compiler_params=pltpu.CompilerParams(vmem_limit_bytes=16 << 20),
        cost_estimate=pl.CostEstimate(
            flops=3_000_000_000, bytes_accessed=2_000_000, transcendentals=4_000_000
        ),
        name="column_physics",
    )(work, got, table, heads, norm_gains, w_qkv, w_out, w_up, w_down, head_t)


def front(place, block_counts, conv_flags, column_state, given, two_bands, weights):
    variables, levels, rows, cols = column_state.shape
    w_embed, level_embed, *arrays = weights
    width = w_embed.shape[1]
    pairs = variables * levels
    depth = -(-(variables + 1) * levels // 64) * 64
    tall = pairs + 8
    wide = given - given % LANES + LANES
    row = shape((pairs, cols))
    outs = [shape((tall, rows * cols)), shape((tall, wide))]
    outs += [row] if two_bands else [row, row]
    outs += [shape((pairs, LANES)), shape((depth, width)), shape((width, width))]
    outs += [shape(w.shape, w.dtype) for w in arrays]
    scratch = [column_state, conv_flags, w_embed, level_embed]
    inputs = scratch + arrays
    hbm = pl.BlockSpec(memory_space=pltpu.HBM)
    return pl.pallas_call(
        functools.partial(front_kernel, given, two_bands, len(arrays)),
        out_shape=outs,
        in_specs=[SMEM, SMEM] + [hbm] * len(inputs),
        out_specs=[VMEM] * len(outs),
        scratch_shapes=[pltpu.VMEM(v.shape, v.dtype) for v in scratch]
        + [pltpu.SemaphoreType.DMA((len(inputs),))],
        compiler_params=pltpu.CompilerParams(vmem_limit_bytes=8 << 20),
        name="pack_and_load",
    )(
        place,
        block_counts,
        *(pltpu.with_memory_space_constraint(v, pltpu.HBM) for v in inputs),
    )


def shards(column_state, conv_flags, block_counts, diffusion, *weights):
    variables, levels, rows, cols = column_state.shape
    pairs = variables * levels
    weights = weights[:-1] + (weights[-1].T,)
    tiles, bands = lax.axis_size("tile"), lax.axis_size("band")
    given = cols + 3 * cols // 8
    kept = rows * cols - 2 * given
    assert tiles % 2 == 0 and given % LANES + rows <= LANES
    place = jnp.stack([lax.axis_index("band"), lax.axis_index("tile")]).astype(jnp.int32)
    packed = front(place, block_counts, conv_flags, column_state, given, bands == 2, weights)
    work, give = packed[:2]
    rows_out, (swap, *weights) = (packed[2:3], packed[3:]) if bands == 2 else (packed[2:4], packed[4:])
    table, heads, gains, *weights = weights
    weights = (table, heads, gains, *weights)
    pairing = [(i, i ^ 1) for i in range(tiles)]
    across = [(i, (i + 1 if i % 2 else i - 1) % tiles) for i in range(tiles)]
    got = lax.ppermute(give, "tile", pairing)
    swap = lax.ppermute(swap, "tile", across)
    if bands == 2:
        north = south = lax.ppermute(rows_out[0], "band", [(0, 1), (1, 0)])
    else:
        south = lax.ppermute(rows_out[0], "band", [(i + 1, i) for i in range(bands - 1)])
        north = lax.ppermute(rows_out[1], "band", [(i, i + 1) for i in range(bands - 1)])
    a = network(0, given, given, work, got, weights, (variables, levels))
    back = lax.ppermute(a, "tile", pairing)
    b = network(1, kept, given, work, got, weights, (variables, levels))

    def kernel(place_ref, *refs):
        final_kernel(place_ref, bands, *refs)

    return pl.pallas_call(
        kernel,
        out_shape=shape(column_state.shape, f32),
        in_specs=[SMEM] + [VMEM] * 10,
        out_specs=pl.BlockSpec(memory_space=pltpu.HBM),
        scratch_shapes=[
            pltpu.VMEM((pairs, rows * cols), bf16),
            pltpu.VMEM(column_state.shape, f32),
            pltpu.SemaphoreType.DMA((2,)),
        ],
        compiler_params=pltpu.CompilerParams(vmem_limit_bytes=8 << 20),
        name="combine",
    )(place, column_state, diffusion, work, got, a, b, back, south, north, swap)


def solution(mesh):
    placed = (
        P(None, None, "band", "tile"),
        P("band", "tile"),
        P("band", "tile"),
        P(),
        P(),
        P(),
        P(),
        P(),
        P(),
        P(),
        P(),
        P(),
    )
    return jax.shard_map(
        shards, mesh=mesh, in_specs=placed, out_specs=P(None, None, "band", "tile"), check_vma=False
    )
```

```python
import functools

import jax
import jax.numpy as jnp
from jax import lax
from jax.experimental import pallas as pl
from jax.experimental.pallas import tpu as pltpu
from jax.sharding import PartitionSpec as P

HEADS = 4
CHAIN = 32
CHAINS = 6
GROUP = 8
LANES = 128
bf16 = jnp.bfloat16
f32 = jnp.float32


def dot(a, b):
    return jnp.dot(a, b, preferred_element_type=f32)


def dot_nt(a, b):
    return lax.dot_general(a, b, (((1,), (1,)), ((), ())), preferred_element_type=f32)


def iota(shape, dim):
    return lax.broadcasted_iota(jnp.int32, shape, dim)


def rms(values, gain):
    mean = jnp.mean(values * values, axis=-1, keepdims=True)
    return values * lax.rsqrt(mean + 1e-05) * gain


def front_kernel(given, two_bands, count, *refs):
    band_ref, tile_ref, count_ref = refs[:3]
    place_ref = (band_ref[0, 0], tile_ref[0, 0])
    sources = refs[3 : 7 + count]
    refs = refs[7 + count :]
    work_ref, give_ref = refs[:2]
    south_ref, north_ref = (None, refs[2]) if two_bands else refs[2:4]
    refs = refs[3 if two_bands else 4 :]
    swap_ref, table_ref, heads_ref = refs[:3]
    loaded = refs[3 : 3 + count]
    x_ref, flags_ref, embed_ref, level_ref, sems = refs[3 + count :]
    targets = (x_ref, flags_ref, embed_ref, level_ref, *loaded)
    copies = [
        pltpu.make_async_copy(source, target, sems.at[i])
        for i, (source, target) in enumerate(zip(sources, targets))
    ]
    for copy in copies:
        copy.start()
    copies[1].wait()
    copies[0].wait()
    pack_rows(
        given, place_ref, count_ref, flags_ref, x_ref, work_ref, give_ref, south_ref, north_ref,
        swap_ref,
    )
    copies[2].wait()
    copies[3].wait()
    build_tables(embed_ref, level_ref, table_ref, heads_ref)
    for copy in copies[4:]:
        copy.wait()


def build_tables(embed_ref, level_ref, table_ref, heads_ref):
    variables, levels = embed_ref.shape[0], level_ref.shape[0]
    depth, width = table_ref.shape
    pairs = variables * levels
    head_size = width // HEADS
    for f in range(variables):
        table_ref[f * levels : (f + 1) * levels, :] = jnp.broadcast_to(
            embed_ref[f : f + 1, :].astype(f32), (levels, width)
        ).astype(bf16)
    table_ref[pairs : pairs + levels, :] = level_ref[...]
    table_ref[pairs + levels :, :] = jnp.zeros((depth - pairs - levels, width), bf16)
    same = iota((width, width), 0) // head_size == iota((width, width), 1) // head_size
    heads_ref[...] = jnp.where(same, 1.0 / head_size, 0.0).astype(bf16)


def pack_rows(
    given, place_ref, count_ref, flags_ref, x_ref, work_ref, give_ref, south_ref, north_ref, swap_ref
):
    variables, levels, rows, cols = x_ref.shape
    pairs = variables * levels
    live = (flags_ref[...] == 1) & (iota((rows, cols), 0) < count_ref[0, 0])
    live = jnp.where(live, 1.0, 0.0)
    extra = work_ref.shape[0] - pairs
    west, east = [], []
    for y in range(rows):
        here = slice(y * cols, (y + 1) * cols)
        state = x_ref[:, :, y, :].reshape(pairs, cols)
        work_ref[:pairs, here] = state.astype(bf16)
        work_ref[pairs:, here] = jnp.where(
            iota((extra, cols), 0) == 0, live[y : y + 1, :], 0.0
        ).astype(bf16)
        west.append(state[:, :LANES])
        east.append(state[:, cols - LANES :])
    first, last = work_ref[:pairs, :cols], work_ref[:pairs, (rows - 1) * cols :]
    if south_ref is None:
        north_ref[...] = jnp.where(place_ref[0] == 0, last, first)
    else:
        north_ref[...] = last
        south_ref[...] = first
    odd = (place_ref[1] % 2).astype(f32)
    even = 1.0 - odd
    lane = iota((pairs, LANES), 1)
    shift = given % LANES
    lows = jnp.zeros((pairs, LANES), f32)
    highs = jnp.zeros((pairs, LANES), f32)
    for y in range(rows):
        lows = jnp.where(lane == y, pltpu.roll(west[y], y, 1) if y else west[y], lows)
        highs = jnp.where(lane == y, pltpu.roll(east[y], y + 1, 1), highs)
    swap_ref[...] = (lows * even + highs * odd).astype(bf16)
    inner = pltpu.roll(lows * odd + highs * even, shift, 1)
    whole = rows * cols
    give_ref[:, :given] = work_ref[:, whole - given :]
    tail = given - shift
    mixed = jnp.where(lane < shift, give_ref[:pairs, tail:].astype(f32), inner)
    give_ref[:pairs, tail:] = mixed.astype(bf16)
    extra_lane = iota((extra, LANES), 1)
    mask = jnp.where(extra_lane < shift, give_ref[pairs:, tail:].astype(f32), 0.0)
    give_ref[pairs:, tail:] = mask.astype(bf16)


def network_kernel(
    phase,
    dims,
    given,
    work_ref,
    got_ref,
    table_sc,
    heads_sc,
    gains_ref,
    qkv_ref,
    out_w_ref,
    up_ref,
    down_ref,
    head_ref,
    phys_ref,
    inputs_sc,
    pos_sc,
):
    variables, levels = dims
    width = out_w_ref.shape[0]
    cols = phys_ref.shape[1]
    head_size = width // HEADS
    pairs = variables * levels
    depth = inputs_sc.shape[0]
    tokens = levels * CHAIN
    group_tokens = levels * GROUP
    zero = jnp.zeros((), bf16)

    before = jnp.where(iota((cols, cols), 0) < iota((cols, cols), 1), 1.0, 0.0).astype(bf16)
    inputs_sc[pairs:, :] = jnp.where(
        iota((depth - pairs, cols), 0) < levels, 1.0, 0.0
    ).astype(bf16)

    def sum_of(source, start):
        return jnp.sum(source[pairs:, start : start + cols].astype(f32)).astype(jnp.int32)

    helped = jnp.sum(got_ref[pairs:, :].astype(f32)).astype(jnp.int32)
    helping = helped > 0
    if phase == 0:
        choices = ((got_ref, 0), (work_ref, 0))
        total_live = jnp.where(helping, helped, sum_of(work_ref, 0))
    else:
        choices = ((work_ref, 0), (work_ref, given))
        total_live = jnp.where(helping, sum_of(work_ref, 0), sum_of(work_ref, given))

    def take(source, start):
        inputs_sc[:pairs, :] = source[:pairs, start : start + cols]
        pos_sc[...] = source[pairs:, start : start + cols].astype(f32)

    pl.when(helping)(functools.partial(take, *choices[0]))
    pl.when(jnp.logical_not(helping))(functools.partial(take, *choices[1]))
    live = pos_sc[...]
    place = dot(live.astype(bf16), before)
    pos_sc[...] = jnp.where(live > 0.5, place, -1.0)
    phys_ref[...] = jnp.zeros(phys_ref.shape, phys_ref.dtype)
    def embed(packed):
        lane_level = iota((levels, depth), 1) % levels
        parts = []
        for g in range(CHAIN // GROUP):
            rows_g = packed[g * GROUP : (g + 1) * GROUP, :]
            for l in range(levels):
                parts.append(jnp.where(lane_level == l, rows_g, 0.0))
        return dot(jnp.concatenate(parts, axis=0).astype(bf16), table_sc[...])

    def project(hidden):
        normed = rms(hidden, gains_ref[0:1, :]).astype(bf16)
        queries = dot(normed, qkv_ref[:, :width])
        keys = dot(normed, qkv_ref[:, width : 2 * width])
        values = dot(normed, qkv_ref[:, 2 * width :]).astype(bf16)
        return queries, keys, values

    def normalize(queries, keys):
        both = jnp.concatenate([queries, keys], axis=0)
        mean = dot((both * both).astype(bf16), heads_sc[...])
        q_mean, k_mean = mean[:tokens], mean[tokens:]
        queries = (queries * (lax.rsqrt(q_mean + 1e-05) * head_size**-0.5)).astype(bf16)
        keys = (keys * lax.rsqrt(k_mean + 1e-05)).astype(bf16)
        return queries, keys

    def split(part):
        head_of = iota((group_tokens, width), 1) // head_size
        return jnp.concatenate(
            [jnp.where(head_of == h, part, zero) for h in range(HEADS)], axis=0
        )

    def attend(parts):
        same = (iota((group_tokens, width), 0) % GROUP) == (iota((group_tokens, width), 1) % GROUP)
        groups = [
            (c, slice(g * group_tokens, (g + 1) * group_tokens))
            for c in range(len(parts))
            for g in range(CHAIN // GROUP)
        ]
        scores = [dot_nt(parts[c][0][h], split(parts[c][1][h])) for c, h in groups]
        probs = [jnp.where(same, jnp.exp(v), 0.0).astype(bf16) for v in scores]
        mixed = [dot(p, split(parts[c][2][h])) for p, (c, h) in zip(probs, groups)]
        total = dot(jnp.concatenate(probs, axis=0), heads_sc[...]) * head_size
        mixed = (jnp.concatenate(mixed, axis=0) / total).astype(bf16)
        return [mixed[c * tokens : (c + 1) * tokens] for c in range(len(parts))]

    def feed(after_attn):
        normed = (rms(after_attn, gains_ref[1:2, :]) * 0.5).astype(bf16)
        inner = dot(normed, up_ref[...])
        inner = (inner + inner * jnp.tanh(inner)).astype(bf16)
        return after_attn + dot(inner, down_ref[...])

    def finish(after_mlp):
        normed = rms(after_mlp, gains_ref[2:3, :]).astype(bf16)
        tend = dot_nt(head_ref[...], normed)
        level_of = (iota((levels, tokens), 1) // GROUP) % levels == iota((levels, tokens), 0)
        return jnp.concatenate(
            [
                jnp.where(level_of, jnp.broadcast_to(tend[f : f + 1, :], (levels, tokens)), 0.0)
                for f in range(variables)
            ],
            axis=0,
        ).astype(bf16)

    def evaluate(start, chains):
        slots = (iota((chains * CHAIN, cols), 0) + start).astype(f32)
        pick = jnp.where(pos_sc[0:1, :] == slots, 1.0, 0.0)
        packed = dot_nt(pick.astype(bf16), inputs_sc[...])
        span = range(chains)
        hidden = [embed(packed[i * CHAIN : (i + 1) * CHAIN, :]) for i in span]
        qkv = [project(h) for h in hidden]
        qk = [normalize(q, k) for q, k, _ in qkv]
        mixed = attend([(*qk[i], qkv[i][2]) for i in span])
        after = [hidden[i] + dot(mixed[i], out_w_ref[...]) for i in span]
        after = [feed(a) for a in after]
        placed = jnp.concatenate([finish(a) for a in after], axis=1)
        parts = []
        for g in range(chains * CHAIN // GROUP):
            part = pick[g * GROUP : (g + 1) * GROUP, :]
            part = jnp.concatenate([part, part], axis=0).astype(bf16)
            parts.extend([part] * (levels // 2))
        phys_ref[...] += dot(placed, jnp.concatenate(parts, axis=0)).astype(phys_ref.dtype)

    units = (total_live + (CHAIN - 1)) // CHAIN
    rounds = (units + 1) // CHAINS

    def body(t, carry):
        evaluate(t * (CHAIN * CHAINS), CHAINS)
        return carry

    lax.fori_loop(0, rounds, body, 0)
    rest = units - rounds * CHAINS
    for chains in range(2, CHAINS - 1, 2):
        pl.when((rest == chains) | (rest == chains - 1))(
            functools.partial(evaluate, rounds * (CHAIN * CHAINS), chains)
        )


def final_kernel(
    place_ref, bands, x_ref, diffusion_ref, work_ref, got_ref, a_ref, b_ref, back_ref,
    south_ref, north_ref, swap_ref, out_ref, phys_sc, result_sc, sems,
):
    variables, levels, rows, cols = x_ref.shape
    pairs = variables * levels
    whole = rows * cols
    na, nb = a_ref.shape[1], b_ref.shape[1]
    helping = jnp.max(got_ref[pairs:, :].astype(f32)) > 0.5

    @pl.when(helping)
    def _():
        phys_sc[:, :nb] = b_ref[...]
        phys_sc[:, nb:] = jnp.zeros((pairs, whole - nb), phys_sc.dtype)

    @pl.when(jnp.logical_not(helping))
    def _():
        phys_sc[:, :na] = a_ref[...]
        phys_sc[:, na : na + nb] = b_ref[...]
        phys_sc[:, na + nb :] = back_ref[...]

    level = iota((levels, levels), 0) == iota((levels, levels), 1)
    rate = jnp.concatenate(
        [
            jnp.sum(
                jnp.where(level, jnp.broadcast_to(diffusion_ref[f : f + 1, :], (levels, levels)), 0.0),
                axis=1,
                keepdims=True,
            )
            for f in range(variables)
        ],
        axis=0,
    )
    state = [x_ref[:, :, y, :].reshape(pairs, cols) for y in range(rows)]
    band = place_ref[0]
    odd = (place_ref[1] % 2).astype(f32)
    even = 1.0 - odd
    shift = na % LANES
    near = pltpu.roll(got_ref[:pairs, na - shift :].astype(f32), LANES - shift, 1)
    far = swap_ref[...].astype(f32)
    west, east = far * even + near * odd, near * even + far * odd
    above = jnp.where(band > 0, north_ref[...].astype(f32), 0.0)
    below = jnp.where(band < bands - 1, south_ref[...].astype(f32), 0.0)
    lane = iota((levels, cols), 1)
    early = variables // 2
    copies = [
        pltpu.make_async_copy(result_sc.at[here], out_ref.at[here], sems.at[i])
        for i, here in enumerate((pl.ds(0, early), pl.ds(early, variables - early)))
    ]
    for f in range(variables):
        part = slice(f * levels, (f + 1) * levels)
        state = [x_ref[f, :, y, :] for y in range(rows)]
        for y in range(rows):
            here = state[y]
            left = jnp.where(lane == 0, west[part, y : y + 1], pltpu.roll(here, 1, 1))
            right = jnp.where(
                lane == cols - 1, east[part, y : y + 1], pltpu.roll(here, cols - 1, 1)
            )
            up = state[y - 1] if y > 0 else above[part]
            down = state[y + 1] if y < rows - 1 else below[part]
            laplace = left + right + up + down - 4.0 * here
            span = slice(y * cols, (y + 1) * cols)
            live = work_ref[pairs : pairs + 1, span].astype(f32) > 0.5
            tend = jnp.where(live, phys_sc[part, span].astype(f32), 0.0)
            result_sc[f, :, y, :] = here + rate[part] * laplace + tend
        if f == variables - 2:
            copies[0].start()
    copies[1].start()
    for copy in copies:
        copy.wait()


VMEM = pl.BlockSpec(memory_space=pltpu.VMEM)
SMEM = pl.BlockSpec(memory_space=pltpu.SMEM)


def shape(dims, dtype=bf16):
    return jax.ShapeDtypeStruct(dims, dtype)


def network(phase, cols, given, work, got, weights, dims):
    variables, levels = dims
    table, heads, norm_gains, w_qkv, w_out, w_up, w_down, head_t = weights
    pairs = variables * levels
    depth = table.shape[0]
    return pl.pallas_call(
        functools.partial(network_kernel, phase, dims, given),
        out_shape=shape((pairs, cols)),
        in_specs=[VMEM] * 10,
        out_specs=VMEM,
        scratch_shapes=[
            pltpu.VMEM((depth, cols), bf16),
            pltpu.VMEM((work.shape[0] - pairs, cols), f32),
        ],
        compiler_params=pltpu.CompilerParams(vmem_limit_bytes=16 << 20),
        cost_estimate=pl.CostEstimate(
            flops=3_000_000_000, bytes_accessed=2_000_000, transcendentals=4_000_000
        ),
        name="column_physics",
    )(work, got, table, heads, norm_gains, w_qkv, w_out, w_up, w_down, head_t)


def front(place, block_counts, conv_flags, column_state, given, two_bands, weights):
    variables, levels, rows, cols = column_state.shape
    w_embed, level_embed, *arrays = weights
    width = w_embed.shape[1]
    pairs = variables * levels
    depth = -(-(variables + 1) * levels // 64) * 64
    tall = pairs + 8
    wide = given - given % LANES + LANES
    row = shape((pairs, cols))
    outs = [shape((tall, rows * cols)), shape((tall, wide))]
    outs += [row] if two_bands else [row, row]
    outs += [shape((pairs, LANES)), shape((depth, width)), shape((width, width))]
    outs += [shape(w.shape, w.dtype) for w in arrays]
    scratch = [column_state, conv_flags, w_embed, level_embed]
    inputs = scratch + arrays
    hbm = pl.BlockSpec(memory_space=pltpu.HBM)
    return pl.pallas_call(
        functools.partial(front_kernel, given, two_bands, len(arrays)),
        out_shape=outs,
        in_specs=[SMEM] * 3 + [hbm] * len(inputs),
        out_specs=[VMEM] * len(outs),
        scratch_shapes=[pltpu.VMEM(v.shape, v.dtype) for v in scratch]
        + [pltpu.SemaphoreType.DMA((len(inputs),))],
        compiler_params=pltpu.CompilerParams(vmem_limit_bytes=8 << 20),
        name="pack_and_load",
    )(
        *place,
        block_counts,
        *(pltpu.with_memory_space_constraint(v, pltpu.HBM) for v in inputs),
    )


def shards(column_state, conv_flags, block_counts, diffusion, *weights):
    variables, levels, rows, cols = column_state.shape
    pairs = variables * levels
    weights = weights[:-1] + (weights[-1].T,)
    tiles, bands = lax.axis_size("tile"), lax.axis_size("band")
    given = cols + 3 * cols // 8
    kept = rows * cols - 2 * given
    assert tiles % 2 == 0 and given % LANES + rows <= LANES
    place = [lax.axis_index(axis).reshape(1, 1).astype(jnp.int32) for axis in ("band", "tile")]
    packed = front(place, block_counts, conv_flags, column_state, given, bands == 2, weights)
    work, give = packed[:2]
    rows_out, (swap, *weights) = (packed[2:3], packed[3:]) if bands == 2 else (packed[2:4], packed[4:])
    table, heads, gains, *weights = weights
    weights = (table, heads, gains, *weights)
    pairing = [(i, i ^ 1) for i in range(tiles)]
    across = [(i, (i + 1 if i % 2 else i - 1) % tiles) for i in range(tiles)]
    got = lax.ppermute(give, "tile", pairing)
    swap = lax.ppermute(swap, "tile", across)
    if bands == 2:
        north = south = lax.ppermute(rows_out[0], "band", [(0, 1), (1, 0)])
    else:
        south = lax.ppermute(rows_out[0], "band", [(i + 1, i) for i in range(bands - 1)])
        north = lax.ppermute(rows_out[1], "band", [(i, i + 1) for i in range(bands - 1)])
    a = network(0, given, given, work, got, weights, (variables, levels))
    back = lax.ppermute(a, "tile", pairing)
    b = network(1, kept, given, work, got, weights, (variables, levels))

    def kernel(band_ref, tile_ref, *refs):
        final_kernel((band_ref[0, 0], tile_ref[0, 0]), bands, *refs)

    return pl.pallas_call(
        kernel,
        out_shape=shape(column_state.shape, f32),
        in_specs=[SMEM] * 2 + [VMEM] * 10,
        out_specs=pl.BlockSpec(memory_space=pltpu.HBM),
        scratch_shapes=[
            pltpu.VMEM((pairs, rows * cols), bf16),
            pltpu.VMEM(column_state.shape, f32),
            pltpu.SemaphoreType.DMA((2,)),
        ],
        compiler_params=pltpu.CompilerParams(vmem_limit_bytes=8 << 20),
        name="combine",
    )(*place, column_state, diffusion, work, got, a, b, back, south, north, swap)


def solution(mesh):
    placed = (
        P(None, None, "band", "tile"),
        P("band", "tile"),
        P("band", "tile"),
        P(),
        P(),
        P(),
        P(),
        P(),
        P(),
        P(),
        P(),
        P(),
    )
    return jax.shard_map(
        shards, mesh=mesh, in_specs=placed, out_specs=P(None, None, "band", "tile"), check_vma=False
    )
```
